512 devices in a mesh: gx: 16 (over x, y_lo), gy: 32 (over z, y_hi, core).
Axes of the slice: x: 4, y: 8 (y_hi: 2, y_lo: 4; y = y_hi * 4 + y_lo), z: 8, core: 2. Of those that a mesh axis runs over, the one named last changes fastest.
Arguments:
- features: bfloat16 [16, 32, 1, 192, 512], P('gx', 'gy'), may hold values from -6 to 6
- occupancy: int32 [16, 32, 1, 512], P('gx', 'gy'), may hold values 0 or 1
- brick_pos: int32 [16, 32, 1], P('gx', 'gy'), may hold values from 0 to 3, as said below
- weight: bfloat16 [192, 27, 192], replicated, may hold values from -0.125 to 0.125
- cotangent: bfloat16 [16, 32, 1, 192, 512], P('gx', 'gy'), may hold values from -6 to 6
Outputs:
- output: bfloat16 [16, 32, 1, 192, 512], P('gx', 'gy')
- x_grad: bfloat16 [16, 32, 1, 192, 512], P('gx', 'gy')
- w_grad: float32 [192, 27, 192], P('gx', None, 'gy')
The draws below stay inside these ranges and needn't reach their ends.
Inputs may be any that keep to these rules, and one draw needn't show every extreme that they name: `brick_pos`: the 1 positions of one device are distinct.
All inputs are finite; a program needn't handle non-finite values. No bound on the sum of `occupancy` on one device may be relied on, other than what follows from the above.
Results may differ from the reference program's by a relative error of at most 0.014.
Values may be sent and summed in bfloat16 or wider, within the bound.
A program may use at most 64 MiB of HBM per device.

```python
import jax
import jax.numpy as jnp
from jax import lax

C = 192
BE = 8
VOX = 512
TX = 2
TY = 2
S = 1
HZ = 1
BRICKS = 512
N_GX = 16
N_GY = 32


def draw_brick_pos(key, part):
    spot_count = TX * TY * HZ
    scores = jax.random.randint(key, (N_GX, N_GY, spot_count), 0, 1048576) * spot_count + jnp.arange(spot_count, dtype=jnp.int32)
    scores = scores.at[0, 0, spot_count - 1].set(-1)
    scores = scores.at[N_GX - 1, N_GY - 1, 0].set(-1)
    ranking = jnp.argsort(scores, axis=-1, stable=True)
    return ranking[:, :, :S].astype(jnp.int32)


def plant(entries, key, smallest, largest):
    place = [jax.random.randint(jax.random.fold_in(key, axis), (), 0, length) for axis, length in enumerate(entries.shape)]
    main_axis = entries.shape.index(max(entries.shape))
    next_to = place[:main_axis] + [(place[main_axis] + 1) % entries.shape[main_axis]] + place[main_axis + 1:]
    return entries.at[tuple(place)].set(smallest).at[tuple(next_to)].set(largest)


def shard_levels(rng, shape, shards, least, high):
    level = 1.0
    for position, parts in shards:
        draws = jax.random.uniform(jax.random.fold_in(jax.random.fold_in(rng, 6), position), (parts,), jnp.float32, least / len(shards), high / len(shards))
        level = level * jnp.repeat(jnp.exp(draws), shape[position] // parts).reshape((-1,) + (1,) * (len(shape) - 1 - position))
    return level


def scatter_about(own_key, shape, deviation, most, cuts=(), kind=jnp.bfloat16):
    gain = shard_levels(own_key, shape, cuts, -0.22, 0.18) if cuts else 1.0
    drawn = jax.random.normal(own_key, shape, jnp.float32) * deviation * gain
    return jnp.minimum(jnp.maximum(drawn, -most), most).astype(kind)


def setup_inputs(seed: int = 0) -> dict:
    seeds = jax.random.split(jax.random.key(seed), 6)
    return {
        "features": scatter_about(seeds[0], (N_GX, N_GY, S, C, VOX), 1.0, 6.0, ((0, 16), (1, 32))),
        "occupancy": plant((jax.random.randint(seeds[1], (N_GX, N_GY, S, VOX), 0, 2) < 1).astype(jnp.int32), jax.random.fold_in(seeds[1], 1), 0, 1),
        "brick_pos": draw_brick_pos(jax.random.fold_in(seeds[5], 71), 0),
        "weight": scatter_about(seeds[3], (C, 27, C), (27 * C // 2) ** -0.5, 0.125),
        "cotangent": scatter_about(seeds[4], (N_GX, N_GY, S, C, VOX), 1.0, 6.0, ((0, 16), (1, 32))),
    }


def tap_windows(window, flipped):
    channels = window.shape[0]
    pieces = []
    for tap_x in range(3):
        for tap_y in range(3):
            for tap_z in range(3):
                if flipped:
                    start_x, start_y, start_z = 2 - tap_x, 2 - tap_y, 2 - tap_z
                else:
                    start_x, start_y, start_z = tap_x, tap_y, tap_z
                piece_view = window[:, start_x:start_x + BE, start_y:start_y + BE, start_z:start_z + BE]
                pieces.append(piece_view.reshape(channels, BE * BE * BE))
    return jnp.stack(pieces, axis=0)


def build_lattice(bricks, brick_x, brick_y, brick_z):
    rows_x, rows_y, slot_count, channels, voxels = bricks.shape
    holder = jnp.zeros((rows_x * TX, rows_y * TY, HZ, channels, BE, BE, BE), bricks.dtype)
    holder = holder.at[brick_x, brick_y, brick_z].set(bricks.reshape(rows_x, rows_y, slot_count, channels, BE, BE, BE))
    lattice = holder.transpose(3, 0, 4, 1, 5, 2, 6).reshape(channels, rows_x * TX * BE, rows_y * TY * BE, HZ * BE)
    return jnp.pad(lattice, ((0, 0), (1, 1), (1, 1), (1, 1)))


def silu_slope(values_in):
    sigma = jax.nn.sigmoid(values_in)
    return sigma * (1.0 + values_in * (1.0 - sigma))


def reference(features, occupancy, brick_pos, weight, cotangent):
    rows_x, rows_y, slot_count, channels, voxels = features.shape
    total = rows_x * rows_y * slot_count
    live_mask = occupancy.astype(jnp.bfloat16)[:, :, :, None, :]
    masked = features * live_mask
    brick_x = (brick_pos // (TY * HZ) + (jnp.arange(rows_x, dtype=jnp.int32) * TX)[:, None, None]).astype(jnp.int32)
    brick_y = ((brick_pos // HZ) % TY + (jnp.arange(rows_y, dtype=jnp.int32) * TY)[None, :, None]).astype(jnp.int32)
    brick_z = (brick_pos % HZ).astype(jnp.int32)
    start_x = (brick_x * BE).reshape(total).astype(jnp.int32)
    start_y = (brick_y * BE).reshape(total).astype(jnp.int32)
    start_z = (brick_z * BE).reshape(total).astype(jnp.int32)
    zero_idx = jnp.zeros((), jnp.int32)
    lattice = build_lattice(masked, brick_x, brick_y, brick_z)
    flat_weight = weight.reshape(channels, 27 * channels)

    def forward_one(brick_index):
        window = lax.dynamic_slice(lattice, (zero_idx, start_x[brick_index], start_y[brick_index], start_z[brick_index]), (channels, BE + 2, BE + 2, BE + 2))
        columns = tap_windows(window, False).reshape(27 * channels, voxels)
        return jnp.dot(flat_weight, columns, preferred_element_type=jnp.float32)

    pre_act = lax.map(forward_one, jnp.arange(total, dtype=jnp.int32)).reshape(features.shape)
    output = (jax.nn.silu(pre_act) * live_mask).astype(jnp.bfloat16)
    slope = (cotangent.astype(jnp.float32) * silu_slope(pre_act) * live_mask).astype(jnp.bfloat16)
    grad_lattice = build_lattice(slope, brick_x, brick_y, brick_z)
    flat_masked = masked.reshape(total, channels, voxels)
    live_flat = live_mask.reshape(total, 1, voxels)
    weight_wide = weight.astype(jnp.float32)

    def backward_one(weight_sum, brick_index):
        window = lax.dynamic_slice(grad_lattice, (zero_idx, start_x[brick_index], start_y[brick_index], start_z[brick_index]), (channels, BE + 2, BE + 2, BE + 2))
        columns = tap_windows(window, True).astype(jnp.float32)
        back_grad = jnp.einsum("okc,kov->cv", weight_wide, columns, precision=lax.Precision.HIGHEST)
        own_input = flat_masked[brick_index].astype(jnp.float32)
        weight_sum = weight_sum + jnp.einsum("kov,cv->okc", columns, own_input, precision=lax.Precision.HIGHEST)
        return weight_sum, (back_grad * live_flat[brick_index]).astype(jnp.bfloat16)

    weight_sum, x_grad = lax.scan(backward_one, jnp.zeros((channels, 27, channels), jnp.float32), jnp.arange(total, dtype=jnp.int32))
    w_grad = weight_sum / BRICKS
    return (output, x_grad.reshape(features.shape), w_grad)
```

```python
import jax
import jax.numpy as jnp
from jax import lax
from jax.sharding import PartitionSpec as P

BE = 8
TX = 2
TY = 2


def extended(block, sides, width):
    for axis, dim in sides:
        count = lax.axis_size(axis)
        forward = [(i, i + 1) for i in range(count - 1)]
        backward = [(target, source) for source, target in forward]
        low = lax.ppermute(
            lax.slice_in_dim(block, block.shape[dim] - width, None, axis=dim), axis, forward
        )
        high = lax.ppermute(lax.slice_in_dim(block, 0, width, axis=dim), axis, backward)
        block = jnp.concatenate([low, block, high], axis=dim)
    return block


def silu_slope(v):
    sigma = jax.nn.sigmoid(v)
    return sigma * (1.0 + v * (1.0 - sigma))


def columns_of(bricks, start, flip):
    channels = bricks.shape[1]
    cube = bricks.reshape(BE, BE, BE, channels)
    zero = jnp.zeros((), jnp.int32)
    lattice = jnp.zeros((TX * BE, TY * BE, BE, channels), bricks.dtype)
    lattice = lax.dynamic_update_slice(lattice, cube, (start[0], start[1], zero, zero))
    wide = extended(lattice, (("gx", 0), ("gy", 1)), 1)
    window = lax.dynamic_slice(
        wide, (start[0], start[1], zero, zero), (BE + 2, BE + 2, BE, channels)
    )
    window = jnp.pad(window, ((0, 0), (0, 0), (1, 1), (0, 0)))
    pieces = []
    for a in range(3):
        for b in range(3):
            for c in range(3):
                s = (2 - a, 2 - b, 2 - c) if flip else (a, b, c)
                view = window[s[0] : s[0] + BE, s[1] : s[1] + BE, s[2] : s[2] + BE, :]
                pieces.append(view.reshape(BE * BE * BE, channels))
    return jnp.concatenate(pieces, axis=1)


def shards(features, occupancy, brick_pos, weight, cotangent):
    x = features[0, 0, 0]
    channels, voxels = x.shape
    mask = occupancy[0, 0].astype(jnp.bfloat16)
    pos = brick_pos[0, 0, 0]
    start = (pos // TY * BE, pos % TY * BE)
    xm = (x * mask).T
    cols = columns_of(xm, start, False)
    w_fwd = weight.reshape(channels, 27 * channels)
    pre = jnp.einsum("ok,vk->ov", w_fwd, cols, preferred_element_type=jnp.float32)
    maskf = mask.astype(jnp.float32)
    output = (jax.nn.silu(pre) * maskf).astype(jnp.bfloat16)
    g = (cotangent[0, 0, 0].astype(jnp.float32) * silu_slope(pre) * maskf).astype(jnp.bfloat16)
    wsum = jnp.einsum("ov,vk->ok", g, cols, preferred_element_type=jnp.float32)
    gcols = columns_of(g.T, start, True)
    w_bwd = weight.transpose(1, 0, 2).reshape(27 * channels, channels)
    back = jnp.einsum("ki,vk->iv", w_bwd, gcols, preferred_element_type=jnp.float32)
    x_grad = (back * maskf).astype(jnp.bfloat16)
    nx, ny = lax.axis_size("gx"), lax.axis_size("gy")
    rows, colw = channels // nx, channels // ny
    part = wsum.astype(jnp.bfloat16).reshape(nx, rows, 27 * channels)
    part = lax.all_to_all(part, "gx", 0, 0)
    part = part.astype(jnp.float32).sum(0)
    part = part.reshape(rows * 27, ny, colw).transpose(1, 0, 2).reshape(ny, rows * 27 * colw)
    part = lax.all_to_all(part.astype(jnp.bfloat16), "gy", 0, 0)
    part = part.astype(jnp.float32).sum(0)
    w_grad = part.reshape(rows, 27, colw) / (nx * ny)
    return (output[None, None, None], x_grad[None, None, None], w_grad)


def solution(mesh):
    placed = (
        P("gx", "gy", None, None, None),
        P("gx", "gy", None, None),
        P("gx", "gy", None),
        P(),
        P("gx", "gy", None, None, None),
    )
    return jax.shard_map(
        shards,
        mesh=mesh,
        in_specs=placed,
        out_specs=(
            P("gx", "gy", None, None, None),
            P("gx", "gy", None, None, None),
            P("gx", None, "gy"),
        ),
        check_vma=False,
    )
```

```python
import jax
import jax.numpy as jnp
from jax import lax
from jax.experimental import pallas as pl
from jax.experimental.pallas import tpu as pltpu
from jax.sharding import PartitionSpec as P

MESH = pl.DeviceIdType.MESH
HALF = 14
BE = 8
TX = 2
TY = 2


def extended(block, sides, width):
    for axis, dim in sides:
        count = lax.axis_size(axis)
        forward = [(i, i + 1) for i in range(count - 1)]
        backward = [(target, source) for source, target in forward]
        low = lax.ppermute(
            lax.slice_in_dim(block, block.shape[dim] - width, None, axis=dim), axis, forward
        )
        high = lax.ppermute(lax.slice_in_dim(block, 0, width, axis=dim), axis, backward)
        block = jnp.concatenate([low, block, high], axis=dim)
    return block


def silu_slope(v):
    sigma = jax.nn.sigmoid(v)
    return sigma * (1.0 + v * (1.0 - sigma))


def columns_of(bricks, start, flip):
    channels = bricks.shape[1]
    cube = bricks.reshape(BE, BE, BE, channels)
    zero = jnp.zeros((), jnp.int32)
    lattice = jnp.zeros((TX * BE, TY * BE, BE, channels), bricks.dtype)
    lattice = lax.dynamic_update_slice(lattice, cube, (start[0], start[1], zero, zero))
    wide = extended(lattice, (("gx", 0), ("gy", 1)), 1)
    window = lax.dynamic_slice(
        wide, (start[0], start[1], zero, zero), (BE + 2, BE + 2, BE, channels)
    )
    window = jnp.pad(window, ((0, 0), (0, 0), (1, 1), (0, 0)))
    pieces = []
    for a in range(3):
        for b in range(3):
            for c in range(3):
                s = (2 - a, 2 - b, 2 - c) if flip else (a, b, c)
                view = window[s[0] : s[0] + BE, s[1] : s[1] + BE, s[2] : s[2] + BE, :]
                pieces.append(view.reshape(BE * BE * BE, channels))
    return jnp.concatenate(pieces, axis=1)


def scatter_kernel(
    part, out, core_rx, mid, x_rx, acc, yb, y_rx, flat, rows, turned, zb, z_rx,
    core_send, core_recv, x_send, x_recv, y_send, y_recv, z_send, z_recv, fin_send, fin_recv,
):
    gx, gy = lax.axis_index("gx"), lax.axis_index("gy")
    x, y = lax.div(gx, 4), lax.rem(gx, 4)
    q, core = lax.div(gy, 2), lax.rem(gy, 2)
    other = 1 - core
    partner = (gx, 2 * q + other)
    x_of = [lax.rem(x + k, 4) for k in range(4)]
    y_of = [lax.rem(y + k, 4) for k in range(4)]
    q_of = [lax.rem(q + k, 16) for k in range(16)]
    x_peer = [(4 * x_of[k] + y, gy) for k in range(4)]
    y_peer = [(4 * x + y_of[k], gy) for k in range(4)]
    q_peer = [(gx, 2 * q_of[k] + core) for k in range(16)]

    barrier = pltpu.get_barrier_semaphore()
    peers = [partner] + x_peer[1:] + y_peer[1:] + q_peer[1:]
    for peer in peers:
        pl.semaphore_signal(barrier, inc=1, device_id=peer, device_id_type=MESH)
    pl.semaphore_wait(barrier, len(peers))

    def remote(src, dst, send, recv, peer):
        return pltpu.make_async_remote_copy(
            src_ref=src, dst_ref=dst, send_sem=send, recv_sem=recv,
            device_id=peer, device_id_type=MESH,
        )

    order = (2, 1, 3, 0)
    core_copy = {
        k: remote(
            part.at[other, x_of[k]], core_rx.at[x_of[k]], core_send.at[k], core_recv.at[k], partner
        )
        for k in order
    }
    for k in order:
        core_copy[k].start()
    x_copy = {
        k: remote(mid.at[x_of[k]], x_rx.at[k - 1], x_send.at[k - 1], x_recv.at[k - 1], x_peer[k])
        for k in (2, 1, 3)
    }
    acc[48:56, :] = jnp.zeros((8, acc.shape[1]), jnp.float32)
    rows[...] = jnp.zeros(rows.shape, jnp.float32)
    for k in order:
        core_copy[k].wait_recv()
        total = part[core, x_of[k]].astype(jnp.float32) + core_rx[x_of[k]].astype(jnp.float32)
        if k:
            mid[x_of[k]] = total.astype(jnp.bfloat16)
            x_copy[k].start()
        else:
            acc[0:48, :] = total
    for k in (1, 3, 2):
        x_copy[k].wait_recv()
        acc[0:48, :] += x_rx[k - 1].astype(jnp.float32)
    for j in range(4):
        yb[j] = acc[12 * j : 12 * j + 16, :].astype(jnp.bfloat16)
    y_copy = {
        k: remote(yb.at[y_of[k]], y_rx.at[k - 1], y_send.at[k - 1], y_recv.at[k - 1], y_peer[k])
        for k in (2, 1, 3)
    }
    for k in (2, 1, 3):
        y_copy[k].start()
    total = yb[y].astype(jnp.float32)
    for k in (1, 3, 2):
        y_copy[k].wait_recv()
        total = total + y_rx[k - 1].astype(jnp.float32)
    flat[...] = total
    width = flat.shape[1] // HALF
    for t in range(HALF):
        rows[16 * t : 16 * t + 16, 0:width] = flat[:, width * t : width * t + width]
    turned[...] = rows[...].T
    for j in range(16):
        zb[j] = turned[12 * j : 12 * j + 16, :].astype(jnp.bfloat16)
    z_copy = [
        remote(zb.at[q_of[k]], z_rx.at[k - 1], z_send.at[k - 1], z_recv.at[k - 1], q_peer[k])
        for k in range(1, 16)
    ]
    for copy in z_copy:
        copy.start()
    total = zb[q].astype(jnp.float32)
    for k, copy in enumerate(z_copy):
        copy.wait_recv()
        total = total + z_rx[k].astype(jnp.float32)
    out[core] = total
    last = remote(out.at[core], out.at[core], fin_send, fin_recv, partner)
    last.start()
    for k in order:
        core_copy[k].wait_send()
    for k in (2, 1, 3):
        x_copy[k].wait_send()
        y_copy[k].wait_send()
    for copy in z_copy:
        copy.wait_send()
    last.wait()


def scattered(part):
    depth = part.shape[3]
    bf, f32 = jnp.bfloat16, jnp.float32
    dma = pltpu.SemaphoreType.DMA
    return pl.pallas_call(
        scatter_kernel,
        out_shape=jax.ShapeDtypeStruct((2, 16, 256), f32),
        in_specs=[pl.BlockSpec(memory_space=pltpu.VMEM)],
        out_specs=pl.BlockSpec(memory_space=pltpu.VMEM),
        scratch_shapes=[
            pltpu.VMEM((4, 48, depth), bf),
            pltpu.VMEM((4, 48, depth), bf),
            pltpu.VMEM((3, 48, depth), bf),
            pltpu.VMEM((56, depth), f32),
            pltpu.VMEM((4, 16, depth), bf),
            pltpu.VMEM((3, 16, depth), bf),
            pltpu.VMEM((16, depth), f32),
            pltpu.VMEM((256, 256), f32),
            pltpu.VMEM((256, 256), f32),
            pltpu.VMEM((16, 16, 256), bf),
            pltpu.VMEM((15, 16, 256), bf),
            dma((4,)), dma((4,)), dma((3,)), dma((3,)), dma((3,)), dma((3,)),
            dma((15,)), dma((15,)), dma, dma,
        ],
        compiler_params=pltpu.CompilerParams(collective_id=0, has_side_effects=True),
    )(part)


def shards(features, occupancy, brick_pos, weight, cotangent):
    x = features[0, 0, 0]
    channels, voxels = x.shape
    mask = occupancy[0, 0].astype(jnp.bfloat16)
    pos = brick_pos[0, 0, 0]
    start = (pos // TY * BE, pos % TY * BE)
    xm = (x * mask).T
    cols = columns_of(xm, start, False)
    w_fwd = weight.reshape(channels, 27 * channels)
    pre = jnp.einsum("ok,vk->ov", w_fwd, cols, preferred_element_type=jnp.float32)
    maskf = mask.astype(jnp.float32)
    output = (jax.nn.silu(pre) * maskf).astype(jnp.bfloat16)
    g = (cotangent[0, 0, 0].astype(jnp.float32) * silu_slope(pre) * maskf).astype(jnp.bfloat16)
    gcols = columns_of(g.T, start, True)
    cut = HALF * channels
    low = jnp.einsum("ov,vk->ok", g, cols[:, :cut], preferred_element_type=jnp.float32)
    high = jnp.einsum("ov,vk->ok", g, cols[:, cut:], preferred_element_type=jnp.float32)
    high = jnp.pad(high, ((0, 0), (0, 2 * cut - 27 * channels)))
    part = jnp.stack([low, high]).astype(jnp.bfloat16).reshape(2, 4, 48, cut)
    part, gcols = lax.optimization_barrier((part, gcols))
    w_bwd = weight.transpose(1, 0, 2).reshape(27 * channels, channels)
    back = jnp.einsum("ki,vk->iv", w_bwd, gcols, preferred_element_type=jnp.float32)
    x_grad = (back * maskf).astype(jnp.bfloat16)
    total = scattered(part)
    mine = lax.dynamic_slice(total, (0, lax.axis_index("gy") % 2 * 6, 0), (2, 6, 16 * HALF))
    mine = mine.reshape(2, 6, HALF, 16)[:, :, :, :12].transpose(3, 0, 2, 1)
    w_grad = mine.reshape(12, 2 * HALF, 6)[:, :27] / (lax.axis_size("gx") * lax.axis_size("gy"))
    return (output[None, None, None], x_grad[None, None, None], w_grad)


def solution(mesh):
    placed = (
        P("gx", "gy", None, None, None),
        P("gx", "gy", None, None),
        P("gx", "gy", None),
        P(),
        P("gx", "gy", None, None, None),
    )
    return jax.shard_map(
        shards,
        mesh=mesh,
        in_specs=placed,
        out_specs=(
            P("gx", "gy", None, None, None),
            P("gx", "gy", None, None, None),
            P("gx", None, "gy"),
        ),
        check_vma=False,
    )
```

```python
import jax
import jax.numpy as jnp
from jax import lax
from jax.experimental import pallas as pl
from jax.experimental.pallas import tpu as pltpu
from jax.sharding import PartitionSpec as P

MESH = pl.DeviceIdType.MESH
HALF = 14
BE = 8
TX = 2
TY = 2


def extended(block, sides, width):
    for axis, dim in sides:
        count = lax.axis_size(axis)
        forward = [(i, i + 1) for i in range(count - 1)]
        backward = [(target, source) for source, target in forward]
        low = lax.ppermute(
            lax.slice_in_dim(block, block.shape[dim] - width, None, axis=dim), axis, forward
        )
        high = lax.ppermute(lax.slice_in_dim(block, 0, width, axis=dim), axis, backward)
        block = jnp.concatenate([low, block, high], axis=dim)
    return block


def window_of(bricks, start):
    channels = bricks.shape[1]
    cube = bricks.reshape(BE, BE, BE, channels)
    zero = jnp.zeros((), jnp.int32)
    lattice = jnp.zeros((TX * BE, TY * BE, BE, channels), bricks.dtype)
    lattice = lax.dynamic_update_slice(lattice, cube, (start[0], start[1], zero, zero))
    wide = extended(lattice, (("gx", 0), ("gy", 1)), 1)
    window = lax.dynamic_slice(
        wide, (start[0], start[1], zero, zero), (BE + 2, BE + 2, BE, channels)
    )
    return jnp.pad(window.astype(jnp.float32), ((0, 0), (0, 0), (0, 0), (0, 256 - channels)))


def shifted(win, zs, odd):
    flat = win[...].reshape(800, 256)
    row = lax.broadcasted_iota(jnp.int32, flat.shape, 0) & 7
    below = jnp.where(row == 0, 0.0, pltpu.roll(flat, 1, 0))
    above = jnp.where(row == 7, 0.0, pltpu.roll(flat, 799, 0))
    for c, value in enumerate((below, flat, above)):
        zs[c] = value.reshape(10, 10, 8, 256)
        odd[c] = pltpu.roll(value, 64, 1).reshape(10, 10, 8, 256)


def tap_view(ref, tap, flip):
    a, b, c = tap // 9, tap // 3 % 3, tap % 3
    if flip:
        a, b, c = 2 - a, 2 - b, 2 - c
    return ref[c, a : a + BE, b : b + BE].reshape(512, 256)


def fill_columns(cols, zs, odd, flip):
    for pair in range(HALF):
        at = 384 * pair
        even = tap_view(zs, 2 * pair, flip)
        cols[:, at : at + 128] = even[:, :128].astype(jnp.bfloat16)
        if pair < HALF - 1:
            late = tap_view(odd, 2 * pair + 1, flip)
            cols[:, at + 128 : at + 256] = (even[:, 128:] + late[:, :128]).astype(jnp.bfloat16)
            cols[:, at + 256 : at + 384] = late[:, 128:].astype(jnp.bfloat16)
        else:
            cols[:, at + 128 : at + 256] = even[:, 128:].astype(jnp.bfloat16)
            cols[:, at + 256 : at + 384] = jnp.zeros((512, 128), jnp.bfloat16)


def dot_nt(left, right):
    return lax.dot_general(
        left, right, (((1,), (1,)), ((), ())), preferred_element_type=jnp.float32
    )


def forward_kernel(win, w_fwd, cot, mask, output, g_out, part, zs, odd, cols):
    shifted(win, zs, odd)
    fill_columns(cols, zs, odd, False)
    pre = dot_nt(w_fwd[...], cols[...])
    sigma = 1.0 / (1.0 + jnp.exp(-pre))
    keep = mask[...]
    output[...] = (pre * sigma * keep).astype(jnp.bfloat16)
    slope = sigma * (1.0 + pre * (1.0 - sigma))
    g = (cot[...].astype(jnp.float32) * slope * keep).astype(jnp.bfloat16)
    g_out[...] = g
    depth = part.shape[3]
    for h in range(2):
        grad = jnp.dot(
            g, cols[:, depth * h : depth * h + depth], preferred_element_type=jnp.float32
        )
        part[h] = grad.astype(jnp.bfloat16).reshape(part.shape[1:])


VMEM_SPEC = pl.BlockSpec(memory_space=pltpu.VMEM)
SHIFT_SCRATCH = [
    pltpu.VMEM((3, 10, 10, 8, 256), jnp.float32),
    pltpu.VMEM((3, 10, 10, 8, 256), jnp.float32),
    pltpu.VMEM((512, 384 * HALF), jnp.bfloat16),
]


def forward(win, w_fwd, cot, mask):
    channels, voxels = cot.shape
    plane = jax.ShapeDtypeStruct((channels, voxels), jnp.bfloat16)
    return pl.pallas_call(
        forward_kernel,
        out_shape=(
            plane, plane, jax.ShapeDtypeStruct((2, 4, 48, HALF * channels), jnp.bfloat16)
        ),
        in_specs=[VMEM_SPEC] * 4,
        out_specs=(VMEM_SPEC,) * 3,
        scratch_shapes=SHIFT_SCRATCH,
    )(win, w_fwd, cot, mask)


def scatter_kernel(
    part, win, w_bwd, mask, out, x_grad, zs, odd, cols, core_rx, mid, x_rx, acc, yb, y_rx, flat, rows, turned, zb, z_rx,
    core_send, core_recv, x_send, x_recv, y_send, y_recv, z_send, z_recv, fin_send, fin_recv,
):
    gx, gy = lax.axis_index("gx"), lax.axis_index("gy")
    x, y = lax.div(gx, 4), lax.rem(gx, 4)
    q, core = lax.div(gy, 2), lax.rem(gy, 2)
    other = 1 - core
    partner = (gx, 2 * q + other)
    x_of = [lax.rem(x + k, 4) for k in range(4)]
    y_of = [lax.rem(y + k, 4) for k in range(4)]
    q_of = [lax.rem(q + k, 16) for k in range(16)]
    x_peer = [(4 * x_of[k] + y, gy) for k in range(4)]
    y_peer = [(4 * x + y_of[k], gy) for k in range(4)]
    q_peer = [(gx, 2 * q_of[k] + core) for k in range(16)]

    barrier = pltpu.get_barrier_semaphore()
    peers = [partner] + x_peer[1:] + y_peer[1:] + q_peer[1:]
    for peer in peers:
        pl.semaphore_signal(barrier, inc=1, device_id=peer, device_id_type=MESH)
    pl.semaphore_wait(barrier, len(peers))

    def remote(src, dst, send, recv, peer):
        return pltpu.make_async_remote_copy(
            src_ref=src, dst_ref=dst, send_sem=send, recv_sem=recv,
            device_id=peer, device_id_type=MESH,
        )

    order = (2, 1, 3, 0)
    core_copy = {
        k: remote(
            part.at[other, x_of[k]], core_rx.at[x_of[k]], core_send.at[k], core_recv.at[k], partner
        )
        for k in order
    }
    for k in order:
        core_copy[k].start()
    x_copy = {
        k: remote(mid.at[x_of[k]], x_rx.at[k - 1], x_send.at[k - 1], x_recv.at[k - 1], x_peer[k])
        for k in (2, 1, 3)
    }
    acc[48:56, :] = jnp.zeros((8, acc.shape[1]), jnp.float32)
    rows[...] = jnp.zeros(rows.shape, jnp.float32)
    for k in order:
        core_copy[k].wait_recv()
        total = part[core, x_of[k]].astype(jnp.float32) + core_rx[x_of[k]].astype(jnp.float32)
        if k:
            mid[x_of[k]] = total.astype(jnp.bfloat16)
            x_copy[k].start()
        else:
            acc[0:48, :] = total
    shifted(win, zs, odd)
    fill_columns(cols, zs, odd, True)
    x_grad[...] = (dot_nt(w_bwd[...], cols[...]) * mask[...]).astype(jnp.bfloat16)
    for k in (1, 3, 2):
        x_copy[k].wait_recv()
        acc[0:48, :] += x_rx[k - 1].astype(jnp.float32)
    for j in range(4):
        yb[j] = acc[12 * j : 12 * j + 16, :].astype(jnp.bfloat16)
    y_copy = {
        k: remote(yb.at[y_of[k]], y_rx.at[k - 1], y_send.at[k - 1], y_recv.at[k - 1], y_peer[k])
        for k in (2, 1, 3)
    }
    for k in (2, 1, 3):
        y_copy[k].start()
    total = yb[y].astype(jnp.float32)
    for k in (1, 3, 2):
        y_copy[k].wait_recv()
        total = total + y_rx[k - 1].astype(jnp.float32)
    flat[...] = total
    width = flat.shape[1] // HALF
    for t in range(HALF):
        rows[16 * t : 16 * t + 16, 0:width] = flat[:, width * t : width * t + width]
    turned[...] = rows[...].T
    for j in range(16):
        zb[j] = turned[12 * j : 12 * j + 16, :].astype(jnp.bfloat16)
    z_copy = [
        remote(zb.at[q_of[k]], z_rx.at[k - 1], z_send.at[k - 1], z_recv.at[k - 1], q_peer[k])
        for k in range(1, 16)
    ]
    for copy in z_copy:
        copy.start()
    total = zb[q].astype(jnp.float32)
    for k, copy in enumerate(z_copy):
        copy.wait_recv()
        total = total + z_rx[k].astype(jnp.float32)
    out[core] = total
    last = remote(out.at[core], out.at[core], fin_send, fin_recv, partner)
    last.start()
    for k in order:
        core_copy[k].wait_send()
    for k in (2, 1, 3):
        x_copy[k].wait_send()
        y_copy[k].wait_send()
    for copy in z_copy:
        copy.wait_send()
    last.wait()


def scattered(part, win, w_bwd, mask):
    depth = part.shape[3]
    bf, f32 = jnp.bfloat16, jnp.float32
    dma = pltpu.SemaphoreType.DMA
    return pl.pallas_call(
        scatter_kernel,
        out_shape=(jax.ShapeDtypeStruct((2, 16, 256), f32), jax.ShapeDtypeStruct((192, 512), bf)),
        in_specs=[VMEM_SPEC] * 4,
        out_specs=(VMEM_SPEC,) * 2,
        scratch_shapes=SHIFT_SCRATCH + [
            pltpu.VMEM((4, 48, depth), bf),
            pltpu.VMEM((4, 48, depth), bf),
            pltpu.VMEM((3, 48, depth), bf),
            pltpu.VMEM((56, depth), f32),
            pltpu.VMEM((4, 16, depth), bf),
            pltpu.VMEM((3, 16, depth), bf),
            pltpu.VMEM((16, depth), f32),
            pltpu.VMEM((256, 256), f32),
            pltpu.VMEM((256, 256), f32),
            pltpu.VMEM((16, 16, 256), bf),
            pltpu.VMEM((15, 16, 256), bf),
            dma((4,)), dma((4,)), dma((3,)), dma((3,)), dma((3,)), dma((3,)),
            dma((15,)), dma((15,)), dma, dma,
        ],
        compiler_params=pltpu.CompilerParams(collective_id=0, has_side_effects=True),
    )(part, win, w_bwd, mask)


def shards(features, occupancy, brick_pos, weight, cotangent):
    x = features[0, 0, 0]
    channels, voxels = x.shape
    mask = occupancy[0, 0].astype(jnp.bfloat16)
    pos = brick_pos[0, 0, 0]
    start = (pos // TY * BE, pos % TY * BE)
    win = window_of((x * mask).T, start)
    maskf = mask.astype(jnp.float32)
    tail = ((0, 0), (0, channels))
    w_fwd = jnp.pad(weight.reshape(channels, 27 * channels), tail)
    w_bwd = jnp.pad(weight.transpose(2, 1, 0).reshape(channels, 27 * channels), tail)
    output, g, part = forward(win, w_fwd, cotangent[0, 0, 0], maskf)
    total, x_grad = scattered(part, window_of(g.T, start), w_bwd, maskf)
    mine = lax.dynamic_slice(total, (0, lax.axis_index("gy") % 2 * 6, 0), (2, 6, 16 * HALF))
    mine = mine.reshape(2, 6, HALF, 16)[:, :, :, :12].transpose(3, 0, 2, 1)
    w_grad = mine.reshape(12, 2 * HALF, 6)[:, :27] / (lax.axis_size("gx") * lax.axis_size("gy"))
    return (output[None, None, None], x_grad[None, None, None], w_grad)


def solution(mesh):
    placed = (
        P("gx", "gy", None, None, None),
        P("gx", "gy", None, None),
        P("gx", "gy", None),
        P(),
        P("gx", "gy", None, None, None),
    )
    return jax.shard_map(
        shards,
        mesh=mesh,
        in_specs=placed,
        out_specs=(
            P("gx", "gy", None, None, None),
            P("gx", "gy", None, None, None),
            P("gx", None, "gy"),
        ),
        check_vma=False,
    )
```

```python
import jax
import jax.numpy as jnp
from jax import lax
from jax.experimental import pallas as pl
from jax.experimental.pallas import tpu as pltpu
from jax.sharding import PartitionSpec as P

MESH = pl.DeviceIdType.MESH
HALF = 14
BE = 8
TY = 2


def shifted(win, zs, odd):
    flat = win[...].reshape(800, 256)
    row = lax.broadcasted_iota(jnp.int32, flat.shape, 0) & 7
    below = jnp.where(row == 0, 0.0, pltpu.roll(flat, 1, 0))
    above = jnp.where(row == 7, 0.0, pltpu.roll(flat, 799, 0))
    for c, value in enumerate((below, flat, above)):
        zs[c] = value.reshape(10, 10, 8, 256)
        odd[c] = pltpu.roll(value, 64, 1).reshape(10, 10, 8, 256)


def tap_view(ref, tap, flip):
    a, b, c = tap // 9, tap // 3 % 3, tap % 3
    if flip:
        a, b, c = 2 - a, 2 - b, 2 - c
    return ref[c, a : a + BE, b : b + BE].reshape(512, 256)


def fill_columns(cols, zs, odd, flip):
    for pair in range(HALF):
        at = 384 * pair
        even = tap_view(zs, 2 * pair, flip)
        cols[:, at : at + 128] = even[:, :128].astype(jnp.bfloat16)
        if pair < HALF - 1:
            late = tap_view(odd, 2 * pair + 1, flip)
            cols[:, at + 128 : at + 256] = (even[:, 128:] + late[:, :128]).astype(jnp.bfloat16)
            cols[:, at + 256 : at + 384] = late[:, 128:].astype(jnp.bfloat16)
        else:
            cols[:, at + 128 : at + 256] = even[:, 128:].astype(jnp.bfloat16)
            cols[:, at + 256 : at + 384] = jnp.zeros((512, 128), jnp.bfloat16)


def dot_nt(left, right):
    return lax.dot_general(
        left, right, (((1,), (1,)), ((), ())), preferred_element_type=jnp.float32
    )


def halo_sends(own, coef, face_tx, line_tx):
    grid = own.reshape(BE, BE, BE, 256)
    faces = (grid[7], grid[0], grid[:, 7], grid[:, 0])
    for d, face in enumerate(faces):
        flat = face.reshape(64, 256)
        both = jnp.concatenate(
            [flat * coef[2 * d : 2 * d + 1, :], flat * coef[2 * d + 1 : 2 * d + 2, :]], axis=0
        )
        face_tx[d] = both.astype(jnp.bfloat16)
    lines = (grid[7, 7], grid[7, 0], grid[0, 7], grid[0, 0])
    for d, line in enumerate(lines):
        line = line * coef[8 + d : 9 + d, :]
        line_tx[d] = jnp.concatenate([line, jnp.zeros_like(line)], axis=0).astype(jnp.bfloat16)


def fill_ring(win, coef, face_rx, line_rx):
    px0, px1, py0, py1 = (coef[12 + d : 13 + d, :] for d in range(4))
    xm, xp, ym, yp = (
        face_rx[d].astype(jnp.float32).reshape(16, BE, 256) for d in range(4)
    )
    mm, mp, pm, pp = (line_rx[d].astype(jnp.float32)[:BE] for d in range(4))
    win[0, 1:9] = px0 * (py0 * xm[:8] + py1 * xm[8:])
    win[9, 1:9] = px1 * (py0 * xp[:8] + py1 * xp[8:])
    win[1:9, 0] = py0 * (px0 * ym[:8] + px1 * ym[8:])
    win[1:9, 9] = py1 * (px0 * yp[:8] + px1 * yp[8:])
    win[0, 0] = py0 * (px0 * mm + px1 * ym[7]) + py1 * (px0 * xm[7])
    win[9, 0] = py0 * (px0 * ym[8] + px1 * pm) + py1 * (px1 * xp[7])
    win[0, 9] = py1 * (px0 * mp + px1 * yp[7]) + py0 * (px0 * xm[8])
    win[9, 9] = py1 * (px0 * yp[8] + px1 * pp) + py0 * (px1 * xp[8])


def voxel_major(value):
    channels, voxels = value.shape
    return jnp.concatenate([value, jnp.zeros((256 - channels, voxels), jnp.float32)], axis=0).T


VMEM_SPEC = pl.BlockSpec(memory_space=pltpu.VMEM)


def fused_kernel(
    feat, cot, mask, coef, weight, output, x_grad, out, win, zs, odd, cols, packed, part,
    face_tx, line_tx, face_rx, line_rx, core_rx, mid, x_rx, acc, yb, y_rx, flat, rows, turned,
    zb, z_rx, face_send, face_recv, line_send, line_recv,
    core_send, core_recv, x_send, x_recv, y_send, y_recv, z_send, z_recv, fin_send, fin_recv,
):
    gx, gy = lax.axis_index("gx"), lax.axis_index("gy")
    x, y = lax.div(gx, 4), lax.rem(gx, 4)
    q, core = lax.div(gy, 2), lax.rem(gy, 2)
    other = 1 - core
    partner = (gx, 2 * q + other)
    x_of = [lax.rem(x + k, 4) for k in range(4)]
    y_of = [lax.rem(y + k, 4) for k in range(4)]
    q_of = [lax.rem(q + k, 16) for k in range(16)]
    x_peer = [(4 * x_of[k] + y, gy) for k in range(4)]
    y_peer = [(4 * x + y_of[k], gy) for k in range(4)]
    q_peer = [(gx, 2 * q_of[k] + core) for k in range(16)]

    nx, ny = lax.axis_size("gx"), lax.axis_size("gy")
    gx_up, gx_down = lax.rem(gx + 1, nx), lax.rem(gx + nx - 1, nx)
    gy_up, gy_down = lax.rem(gy + 1, ny), lax.rem(gy + ny - 1, ny)
    face_peer = [(gx_up, gy), (gx_down, gy), (gx, gy_up), (gx, gy_down)]
    line_peer = [(gx_up, gy_up), (gx_up, gy_down), (gx_down, gy_up), (gx_down, gy_down)]

    barrier = pltpu.get_barrier_semaphore()
    peers = [partner] + x_peer[1:] + y_peer[1:] + q_peer[1:] + face_peer + line_peer
    for peer in peers:
        pl.semaphore_signal(barrier, inc=1, device_id=peer, device_id_type=MESH)
    pl.semaphore_wait(barrier, len(peers))

    def remote(src, dst, send, recv, peer):
        return pltpu.make_async_remote_copy(
            src_ref=src, dst_ref=dst, send_sem=send, recv_sem=recv,
            device_id=peer, device_id_type=MESH,
        )

    def halo(step):
        copies = []
        for d in range(4):
            copies.append(
                remote(
                    face_tx.at[step, d], face_rx.at[step, d],
                    face_send.at[step, d], face_recv.at[step, d], face_peer[d],
                )
            )
            copies.append(
                remote(
                    line_tx.at[step, d], line_rx.at[step, d],
                    line_send.at[step, d], line_recv.at[step, d], line_peer[d],
                )
            )
        return copies

    keep = mask[...]
    bf, f32 = jnp.bfloat16, jnp.float32
    channels = feat.shape[0]
    x_halo, g_halo = halo(0), halo(1)
    own = voxel_major(feat[...].astype(f32) * keep)
    halo_sends(own, coef, face_tx.at[0], line_tx.at[0])
    for copy in x_halo:
        copy.start()
    win[1:9, 1:9] = own.reshape(BE, BE, BE, 256)
    for pair in range(HALF):
        at = 2 * pair * channels
        left = weight[at : at + channels, :]
        if pair < HALF - 1:
            right = weight[at + channels : at + 2 * channels, :]
        else:
            right = jnp.zeros((channels, channels), bf)
        packed[:, at : at + 2 * channels] = jnp.concatenate([left, right], axis=1)
    for copy in x_halo:
        copy.wait_recv()
    fill_ring(win, coef, face_rx.at[0], line_rx.at[0])
    shifted(win, zs, odd)
    fill_columns(cols, zs, odd, False)
    pre = dot_nt(packed[...], cols[...])
    sigma = 1.0 / (1.0 + jnp.exp(-pre))
    output[...] = (pre * sigma * keep).astype(bf)
    slope = sigma * (1.0 + pre * (1.0 - sigma))
    g = (cot[...].astype(f32) * slope * keep).astype(bf)
    own = voxel_major(g.astype(f32))
    halo_sends(own, coef, face_tx.at[1], line_tx.at[1])
    for copy in g_halo:
        copy.start()
    win[1:9, 1:9] = own.reshape(BE, BE, BE, 256)
    depth = part.shape[3]

    def partial(half):
        view = cols[:, pl.ds(pl.multiple_of(half * depth, 128), depth)]
        grad = jnp.dot(g, view, preferred_element_type=f32)
        part[half] = grad.astype(bf).reshape(part.shape[1:])

    partial(other)
    order = (2, 1, 3, 0)
    core_copy = {
        k: remote(
            part.at[other, x_of[k]], core_rx.at[x_of[k]], core_send.at[k], core_recv.at[k], partner
        )
        for k in order
    }
    for k in order:
        core_copy[k].start()
    partial(core)
    x_copy = {
        k: remote(mid.at[x_of[k]], x_rx.at[k - 1], x_send.at[k - 1], x_recv.at[k - 1], x_peer[k])
        for k in (2, 1, 3)
    }
    acc[48:56, :] = jnp.zeros((8, acc.shape[1]), jnp.float32)
    rows[...] = jnp.zeros(rows.shape, jnp.float32)
    for k in order:
        core_copy[k].wait_recv()
        total = part[core, x_of[k]].astype(jnp.float32) + core_rx[x_of[k]].astype(jnp.float32)
        if k:
            mid[x_of[k]] = total.astype(jnp.bfloat16)
            x_copy[k].start()
        else:
            acc[0:48, :] = total
    for copy in g_halo:
        copy.wait_recv()
    fill_ring(win, coef, face_rx.at[1], line_rx.at[1])
    shifted(win, zs, odd)
    fill_columns(cols, zs, odd, True)
    cut, end = 26 * channels, 27 * channels
    back = jnp.dot(cols[:, :cut], weight[:cut, :], preferred_element_type=f32)
    back = back + jnp.dot(cols[:, cut:end], weight[cut:end, :], preferred_element_type=f32)
    wide = jnp.concatenate([back, jnp.zeros((512, 256 - channels), f32)], axis=1)
    x_grad[...] = (wide.T[:channels] * keep).astype(bf)
    for k in (1, 3, 2):
        x_copy[k].wait_recv()
        acc[0:48, :] += x_rx[k - 1].astype(jnp.float32)
    for j in range(4):
        yb[j] = acc[12 * j : 12 * j + 16, :].astype(jnp.bfloat16)
    y_copy = {
        k: remote(yb.at[y_of[k]], y_rx.at[k - 1], y_send.at[k - 1], y_recv.at[k - 1], y_peer[k])
        for k in (2, 1, 3)
    }
    for k in (2, 1, 3):
        y_copy[k].start()
    total = yb[y].astype(jnp.float32)
    for k in (1, 3, 2):
        y_copy[k].wait_recv()
        total = total + y_rx[k - 1].astype(jnp.float32)
    flat[...] = total
    width = flat.shape[1] // HALF
    for t in range(HALF):
        rows[16 * t : 16 * t + 16, 0:width] = flat[:, width * t : width * t + width]
    turned[...] = rows[...].T
    for j in range(16):
        zb[j] = turned[12 * j : 12 * j + 16, :].astype(jnp.bfloat16)
    z_copy = [
        remote(zb.at[q_of[k]], z_rx.at[k - 1], z_send.at[k - 1], z_recv.at[k - 1], q_peer[k])
        for k in range(1, 16)
    ]
    for copy in z_copy:
        copy.start()
    total = zb[q].astype(jnp.float32)
    for k, copy in enumerate(z_copy):
        copy.wait_recv()
        total = total + z_rx[k].astype(jnp.float32)
    out[core] = total
    last = remote(out.at[core], out.at[core], fin_send, fin_recv, partner)
    last.start()
    for k in order:
        core_copy[k].wait_send()
    for k in (2, 1, 3):
        x_copy[k].wait_send()
        y_copy[k].wait_send()
    for copy in z_copy:
        copy.wait_send()
    for copy in x_halo + g_halo:
        copy.wait_send()
    last.wait()


def fused(feat, cot, mask, coef, weight):
    channels, voxels = feat.shape
    depth = HALF * channels
    bf, f32 = jnp.bfloat16, jnp.float32
    dma = pltpu.SemaphoreType.DMA
    plane = jax.ShapeDtypeStruct((channels, voxels), bf)
    return pl.pallas_call(
        fused_kernel,
        out_shape=(plane, plane, jax.ShapeDtypeStruct((2, 16, 256), f32)),
        in_specs=[VMEM_SPEC] * 5,
        out_specs=(VMEM_SPEC,) * 3,
        scratch_shapes=[
            pltpu.VMEM((10, 10, BE, 256), f32),
            pltpu.VMEM((3, 10, 10, BE, 256), f32),
            pltpu.VMEM((3, 10, 10, BE, 256), f32),
            pltpu.VMEM((voxels, 2 * depth), bf),
            pltpu.VMEM((channels, 2 * depth), bf),
            pltpu.VMEM((2, 4, 48, depth), bf),
            pltpu.VMEM((2, 4, 128, 256), bf),
            pltpu.VMEM((2, 4, 16, 256), bf),
            pltpu.VMEM((2, 4, 128, 256), bf),
            pltpu.VMEM((2, 4, 16, 256), bf),
            pltpu.VMEM((4, 48, depth), bf),
            pltpu.VMEM((4, 48, depth), bf),
            pltpu.VMEM((3, 48, depth), bf),
            pltpu.VMEM((56, depth), f32),
            pltpu.VMEM((4, 16, depth), bf),
            pltpu.VMEM((3, 16, depth), bf),
            pltpu.VMEM((16, depth), f32),
            pltpu.VMEM((256, 256), f32),
            pltpu.VMEM((256, 256), f32),
            pltpu.VMEM((16, 16, 256), bf),
            pltpu.VMEM((15, 16, 256), bf),
            dma((2, 4)), dma((2, 4)), dma((2, 4)), dma((2, 4)),
            dma((4,)), dma((4,)), dma((3,)), dma((3,)), dma((3,)), dma((3,)),
            dma((15,)), dma((15,)), dma, dma,
        ],
        compiler_params=pltpu.CompilerParams(collective_id=0, has_side_effects=True),
    )(feat, cot, mask, coef, weight)


def coefficients(pos):
    gx, gy = lax.axis_index("gx"), lax.axis_index("gy")
    px, py = pos // TY == 1, pos % TY == 1
    up_x, up_y = gx < lax.axis_size("gx") - 1, gy < lax.axis_size("gy") - 1
    down_x, down_y = gx > 0, gy > 0
    out_x, in_x = px & up_x, ~px & down_x
    out_y, in_y = py & up_y, ~py & down_y
    flags = [
        out_x & ~py, out_x & py, in_x & ~py, in_x & py,
        out_y & ~px, out_y & px, in_y & ~px, in_y & px,
        out_x & out_y, out_x & in_y, in_x & out_y, in_x & in_y,
        ~px, px, ~py, py,
    ]
    return jnp.broadcast_to(jnp.stack(flags).astype(jnp.float32)[:, None], (16, 256))


def shards(features, occupancy, brick_pos, weight, cotangent):
    mask = occupancy[0, 0].astype(jnp.float32)
    channels = weight.shape[0]
    w2 = weight.transpose(1, 0, 2).reshape(27 * channels, channels)
    output, x_grad, total = fused(
        features[0, 0, 0], cotangent[0, 0, 0], mask, coefficients(brick_pos[0, 0, 0]), w2
    )
    mine = lax.dynamic_slice(total, (0, lax.axis_index("gy") % 2 * 6, 0), (2, 6, 16 * HALF))
    mine = mine.reshape(2, 6, HALF, 16)[:, :, :, :12].transpose(3, 0, 2, 1)
    w_grad = mine.reshape(12, 2 * HALF, 6)[:, :27] / (lax.axis_size("gx") * lax.axis_size("gy"))
    return (output[None, None, None], x_grad[None, None, None], w_grad)


def solution(mesh):
    placed = (
        P("gx", "gy", None, None, None),
        P("gx", "gy", None, None),
        P("gx", "gy", None),
        P(),
        P("gx", "gy", None, None, None),
    )
    return jax.shard_map(
        shards,
        mesh=mesh,
        in_specs=placed,
        out_specs=(
            P("gx", "gy", None, None, None),
            P("gx", "gy", None, None, None),
            P("gx", None, "gy"),
        ),
        check_vma=False,
    )
```

```python
import jax
import jax.numpy as jnp
from jax import lax
from jax.experimental import pallas as pl
from jax.experimental.pallas import tpu as pltpu
from jax.sharding import PartitionSpec as P

MESH = pl.DeviceIdType.MESH
HALF = 14
BE = 8
TY = 2


def shifted(win, zs, odd):
    flat = win[...].reshape(800, 256)
    row = lax.broadcasted_iota(jnp.int32, flat.shape, 0) & 7
    below = jnp.where(row == 0, 0.0, pltpu.roll(flat, 1, 0))
    above = jnp.where(row == 7, 0.0, pltpu.roll(flat, 799, 0))
    for c, value in enumerate((below, flat, above)):
        zs[c] = value.reshape(10, 10, 8, 256)
        odd[c] = pltpu.roll(value, 64, 1).reshape(10, 10, 8, 256)


def tap_view(ref, tap, flip):
    a, b, c = tap // 9, tap // 3 % 3, tap % 3
    if flip:
        a, b, c = 2 - a, 2 - b, 2 - c
    return ref[c, a : a + BE, b : b + BE].reshape(512, 256)


def fill_columns(cols, zs, odd, flip):
    for pair in range(HALF):
        at = 384 * pair
        even = tap_view(zs, 2 * pair, flip)
        cols[:, at : at + 128] = even[:, :128].astype(jnp.bfloat16)
        if pair < HALF - 1:
            late = tap_view(odd, 2 * pair + 1, flip)
            cols[:, at + 128 : at + 256] = (even[:, 128:] + late[:, :128]).astype(jnp.bfloat16)
            cols[:, at + 256 : at + 384] = late[:, 128:].astype(jnp.bfloat16)
        else:
            cols[:, at + 128 : at + 256] = even[:, 128:].astype(jnp.bfloat16)
            cols[:, at + 256 : at + 384] = jnp.zeros((512, 128), jnp.bfloat16)


def dot_nt(left, right):
    return lax.dot_general(
        left, right, (((1,), (1,)), ((), ())), preferred_element_type=jnp.float32
    )


def halo_sends(own, coef, face_tx, line_tx):
    grid = own.reshape(BE, BE, BE, 256)
    faces = (grid[7], grid[0], grid[:, 7], grid[:, 0])
    for d, face in enumerate(faces):
        flat = face.reshape(64, 256)
        both = jnp.concatenate(
            [flat * coef[2 * d], flat * coef[2 * d + 1]], axis=0
        )
        face_tx[d] = both.astype(jnp.bfloat16)
    lines = (grid[7, 7], grid[7, 0], grid[0, 7], grid[0, 0])
    for d, line in enumerate(lines):
        line = line * coef[8 + d]
        line_tx[d] = jnp.concatenate([line, jnp.zeros_like(line)], axis=0).astype(jnp.bfloat16)


def fill_ring(win, coef, face_rx, line_rx):
    px0, px1, py0, py1 = coef[12:16]
    xm, xp, ym, yp = (
        face_rx[d].astype(jnp.float32).reshape(16, BE, 256) for d in range(4)
    )
    mm, mp, pm, pp = (line_rx[d].astype(jnp.float32)[:BE] for d in range(4))
    win[0, 1:9] = px0 * (py0 * xm[:8] + py1 * xm[8:])
    win[9, 1:9] = px1 * (py0 * xp[:8] + py1 * xp[8:])
    win[1:9, 0] = py0 * (px0 * ym[:8] + px1 * ym[8:])
    win[1:9, 9] = py1 * (px0 * yp[:8] + px1 * yp[8:])
    win[0, 0] = py0 * (px0 * mm + px1 * ym[7]) + py1 * (px0 * xm[7])
    win[9, 0] = py0 * (px0 * ym[8] + px1 * pm) + py1 * (px1 * xp[7])
    win[0, 9] = py1 * (px0 * mp + px1 * yp[7]) + py0 * (px0 * xm[8])
    win[9, 9] = py1 * (px0 * yp[8] + px1 * pp) + py0 * (px1 * xp[8])


def voxel_major(value):
    channels, voxels = value.shape
    return jnp.concatenate([value, jnp.zeros((256 - channels, voxels), jnp.float32)], axis=0).T


def coefficients(pos, gx, gy, nx, ny):
    one = jnp.float32(1.0)
    px, py = (pos >> 1).astype(jnp.float32), (pos & 1).astype(jnp.float32)
    qx, qy = one - px, one - py
    out_x = px * (gx < nx - 1).astype(jnp.float32)
    in_x = qx * (gx > 0).astype(jnp.float32)
    out_y = py * (gy < ny - 1).astype(jnp.float32)
    in_y = qy * (gy > 0).astype(jnp.float32)
    return (
        out_x * qy, out_x * py, in_x * qy, in_x * py,
        out_y * qx, out_y * px, in_y * qx, in_y * px,
        out_x * out_y, out_x * in_y, in_x * out_y, in_x * in_y,
        qx, px, qy, py,
    )


VMEM_SPEC = pl.BlockSpec(memory_space=pltpu.VMEM)
HBM_SPEC = pl.BlockSpec(memory_space=pltpu.HBM)
SMEM_SPEC = pl.BlockSpec(memory_space=pltpu.SMEM)


def fused_kernel(
    feat, cot_hbm, mask, pos, weight_hbm, output_hbm, x_grad_hbm, out, cot, weight, output, x_grad,
    local, win, zs, odd, cols, packed, part,
    face_tx, line_tx, face_rx, line_rx, core_rx, mid, x_rx, acc, yb, y_rx, flat, rows, turned,
    zb, z_rx, face_send, face_recv, line_send, line_recv,
    relay, core_send, core_recv, x_send, x_recv, y_send, y_recv, z_send, z_recv, fin_send, fin_recv,
):
    gx, gy = lax.axis_index("gx"), lax.axis_index("gy")
    x, y = lax.div(gx, 4), lax.rem(gx, 4)
    q, core = lax.div(gy, 2), lax.rem(gy, 2)
    other = 1 - core
    partner = (gx, 2 * q + other)
    x_of = [lax.rem(x + k, 4) for k in range(4)]
    y_of = [lax.rem(y + k, 4) for k in range(4)]
    q_of = [lax.rem(q + k, 16) for k in range(16)]
    x_peer = [(4 * x_of[k] + y, gy) for k in range(4)]
    y_peer = [(4 * x + y_of[k], gy) for k in range(4)]
    q_peer = [(gx, 2 * q_of[k] + core) for k in range(16)]

    nx, ny = lax.axis_size("gx"), lax.axis_size("gy")
    gx_up, gx_down = lax.rem(gx + 1, nx), lax.rem(gx + nx - 1, nx)
    gy_up, gy_down = lax.rem(gy + 1, ny), lax.rem(gy + ny - 1, ny)
    face_peer = [(gx_up, gy), (gx_down, gy), (gx, gy_up), (gx, gy_down)]
    line_peer = [(gx_up, gy_up), (gx_up, gy_down), (gx_down, gy_up), (gx_down, gy_down)]

    load_weight = pltpu.make_async_copy(weight_hbm, weight, local.at[0])
    load_cot = pltpu.make_async_copy(cot_hbm, cot, local.at[1])
    save_output = pltpu.make_async_copy(output, output_hbm, local.at[2])
    save_x_grad = pltpu.make_async_copy(x_grad, x_grad_hbm, local.at[3])
    load_weight.start()
    load_cot.start()
    coef = coefficients(pos[0], gx, gy, nx, ny)

    barrier = pltpu.get_barrier_semaphore()
    peers = [partner] + x_peer[1:] + y_peer[1:] + q_peer[1:] + face_peer + line_peer
    for peer in peers:
        pl.semaphore_signal(barrier, inc=1, device_id=peer, device_id_type=MESH)
    pl.semaphore_wait(barrier, len(peers))

    def remote(src, dst, send, recv, peer):
        return pltpu.make_async_remote_copy(
            src_ref=src, dst_ref=dst, send_sem=send, recv_sem=recv,
            device_id=peer, device_id_type=MESH,
        )

    def halo(step):
        copies = []
        for d in range(4):
            copies.append(
                remote(
                    face_tx.at[step, d], face_rx.at[step, d],
                    face_send.at[step, d], face_recv.at[step, d], face_peer[d],
                )
            )
            copies.append(
                remote(
                    line_tx.at[step, d], line_rx.at[step, d],
                    line_send.at[step, d], line_recv.at[step, d], line_peer[d],
                )
            )
        return copies

    keep = mask[...].astype(jnp.float32)
    bf, f32 = jnp.bfloat16, jnp.float32
    channels = feat.shape[0]
    x_halo, g_halo = halo(0), halo(1)
    own = voxel_major(feat[...].astype(f32) * keep)
    halo_sends(own, coef, face_tx.at[0], line_tx.at[0])
    for copy in x_halo:
        copy.start()
    win[1:9, 1:9] = own.reshape(BE, BE, BE, 256)
    load_weight.wait()
    for pair in range(HALF):
        at = 2 * pair * channels
        left = weight[at : at + channels, :]
        if pair < HALF - 1:
            right = weight[at + channels : at + 2 * channels, :]
        else:
            right = jnp.zeros((channels, channels), bf)
        packed[:, at : at + 2 * channels] = jnp.concatenate([left, right], axis=1)
    for copy in x_halo:
        copy.wait_recv()
    fill_ring(win, coef, face_rx.at[0], line_rx.at[0])
    shifted(win, zs, odd)
    fill_columns(cols, zs, odd, False)
    pre = dot_nt(packed[...], cols[...])
    sigma = 1.0 / (1.0 + jnp.exp(-pre))
    output[...] = (pre * sigma * keep).astype(bf)
    save_output.start()
    load_cot.wait()
    slope = sigma * (1.0 + pre * (1.0 - sigma))
    g = (cot[...].astype(f32) * slope * keep).astype(bf)
    own = voxel_major(g.astype(f32))
    halo_sends(own, coef, face_tx.at[1], line_tx.at[1])
    for copy in g_halo:
        copy.start()
    win[1:9, 1:9] = own.reshape(BE, BE, BE, 256)
    depth = part.shape[3]

    def partial(half):
        view = cols[:, pl.ds(pl.multiple_of(half * depth, 128), depth)]
        grad = jnp.dot(g, view, preferred_element_type=f32)
        part[half] = grad.astype(bf).reshape(part.shape[1:])

    partial(other)
    order = (2, 1, 3, 0)
    core_copy = {
        k: remote(
            part.at[other, x_of[k]], core_rx.at[x_of[k]], core_send.at[k], core_recv.at[k], partner
        )
        for k in order
    }
    for k in order:
        core_copy[k].start()
    partial(core)
    depth = part.shape[3]
    cut = 1408
    lanes_a, lanes_b = pl.ds(0, cut), pl.ds(cut, depth - cut)
    far, right, left = x_of[2], x_of[1], x_of[3]
    routes = (
        (mid.at[far, :, lanes_a], relay.at[:, lanes_a], x_peer[1]),
        (mid.at[far, :, lanes_b], relay.at[:, lanes_b], x_peer[3]),
        (mid.at[right, :, lanes_b], x_rx.at[0, :, lanes_b], x_peer[1]),
        (mid.at[left, :, lanes_a], x_rx.at[1, :, lanes_a], x_peer[3]),
        (mid.at[right, :, lanes_a], x_rx.at[0, :, lanes_a], x_peer[1]),
        (mid.at[left, :, lanes_b], x_rx.at[1, :, lanes_b], x_peer[3]),
    )
    x_copy = [
        remote(src, dst, x_send.at[n], x_recv.at[n], peer)
        for n, (src, dst, peer) in enumerate(routes)
    ]

    def pair_sum(d, lanes):
        return part[core, d, :, lanes].astype(f32) + core_rx[d, :, lanes].astype(f32)

    acc[48:56, :] = jnp.zeros((8, acc.shape[1]), jnp.float32)
    rows[...] = jnp.zeros(rows.shape, jnp.float32)
    for k in order:
        core_copy[k].wait_recv()
        if k == 2:
            mid[far] = pair_sum(far, slice(None)).astype(bf)
            x_copy[0].start()
            x_copy[1].start()
        elif k == 1:
            mid[right, :, lanes_b] = pair_sum(right, lanes_b).astype(bf)
            x_copy[2].start()
        elif k == 3:
            mid[left, :, lanes_a] = pair_sum(left, lanes_a).astype(bf)
            x_copy[3].start()
        else:
            acc[0:48, :] = pair_sum(x, slice(None))
    for copy in g_halo:
        copy.wait_recv()
    fill_ring(win, coef, face_rx.at[1], line_rx.at[1])
    shifted(win, zs, odd)
    x_copy[0].wait_recv()
    relayed = pair_sum(right, lanes_a) + relay[:, lanes_a].astype(f32)
    mid[right, :, lanes_a] = relayed.astype(bf)
    x_copy[4].start()
    x_copy[1].wait_recv()
    relayed = pair_sum(left, lanes_b) + relay[:, lanes_b].astype(f32)
    mid[left, :, lanes_b] = relayed.astype(bf)
    x_copy[5].start()
    fill_columns(cols, zs, odd, True)
    cut, end = 26 * channels, 27 * channels
    back = jnp.dot(cols[:, :cut], weight[:cut, :], preferred_element_type=f32)
    back = back + jnp.dot(cols[:, cut:end], weight[cut:end, :], preferred_element_type=f32)
    wide = jnp.concatenate([back, jnp.zeros((512, 256 - channels), f32)], axis=1)
    x_grad[...] = (wide.T[:channels] * keep).astype(bf)
    save_x_grad.start()
    for n in (2, 3, 4, 5):
        x_copy[n].wait_recv()
    acc[0:48, :] += x_rx[0].astype(f32) + x_rx[1].astype(f32)
    for j in range(4):
        yb[j] = acc[12 * j : 12 * j + 16, :].astype(jnp.bfloat16)
    y_copy = {
        k: remote(yb.at[y_of[k]], y_rx.at[k - 1], y_send.at[k - 1], y_recv.at[k - 1], y_peer[k])
        for k in (2, 1, 3)
    }
    for k in (2, 1, 3):
        y_copy[k].start()
    total = yb[y].astype(jnp.float32)
    for k in (1, 3, 2):
        y_copy[k].wait_recv()
        total = total + y_rx[k - 1].astype(jnp.float32)
    flat[...] = total
    width = flat.shape[1] // HALF
    for t in range(HALF):
        rows[16 * t : 16 * t + 16, 0:width] = flat[:, width * t : width * t + width]
    turned[...] = rows[...].T
    for j in range(16):
        zb[j] = turned[12 * j : 12 * j + 16, :].astype(jnp.bfloat16)
    z_copy = [
        remote(zb.at[q_of[k]], z_rx.at[k - 1], z_send.at[k - 1], z_recv.at[k - 1], q_peer[k])
        for k in range(1, 16)
    ]
    for copy in z_copy:
        copy.start()
    total = zb[q].astype(jnp.float32)
    for k, copy in enumerate(z_copy):
        copy.wait_recv()
        total = total + z_rx[k].astype(jnp.float32)
    out[core] = total
    last = remote(out.at[core], out.at[core], fin_send, fin_recv, partner)
    last.start()
    for k in order:
        core_copy[k].wait_send()
    for copy in x_copy:
        copy.wait_send()
    for k in (2, 1, 3):
        y_copy[k].wait_send()
    for copy in z_copy:
        copy.wait_send()
    for copy in x_halo + g_halo:
        copy.wait_send()
    last.wait()
    save_output.wait()
    save_x_grad.wait()


def fused(feat, cot, mask, pos, weight):
    channels, voxels = feat.shape
    depth = HALF * channels
    bf, f32 = jnp.bfloat16, jnp.float32
    dma = pltpu.SemaphoreType.DMA
    plane = jax.ShapeDtypeStruct((channels, voxels), bf)
    return pl.pallas_call(
        fused_kernel,
        out_shape=(plane, plane, jax.ShapeDtypeStruct((2, 16, 256), f32)),
        in_specs=[VMEM_SPEC, HBM_SPEC, VMEM_SPEC, SMEM_SPEC, HBM_SPEC],
        out_specs=(HBM_SPEC, HBM_SPEC, VMEM_SPEC),
        scratch_shapes=[
            pltpu.VMEM((channels, voxels), bf),
            pltpu.VMEM(weight.shape, bf),
            pltpu.VMEM((channels, voxels), bf),
            pltpu.VMEM((channels, voxels), bf),
            dma((4,)),
            pltpu.VMEM((10, 10, BE, 256), f32),
            pltpu.VMEM((3, 10, 10, BE, 256), f32),
            pltpu.VMEM((3, 10, 10, BE, 256), f32),
            pltpu.VMEM((voxels, 2 * depth), bf),
            pltpu.VMEM((channels, 2 * depth), bf),
            pltpu.VMEM((2, 4, 48, depth), bf),
            pltpu.VMEM((2, 4, 128, 256), bf),
            pltpu.VMEM((2, 4, 16, 256), bf),
            pltpu.VMEM((2, 4, 128, 256), bf),
            pltpu.VMEM((2, 4, 16, 256), bf),
            pltpu.VMEM((4, 48, depth), bf),
            pltpu.VMEM((4, 48, depth), bf),
            pltpu.VMEM((2, 48, depth), bf),
            pltpu.VMEM((56, depth), f32),
            pltpu.VMEM((4, 16, depth), bf),
            pltpu.VMEM((3, 16, depth), bf),
            pltpu.VMEM((16, depth), f32),
            pltpu.VMEM((256, 256), f32),
            pltpu.VMEM((256, 256), f32),
            pltpu.VMEM((16, 16, 256), bf),
            pltpu.VMEM((15, 16, 256), bf),
            dma((2, 4)), dma((2, 4)), dma((2, 4)), dma((2, 4)),
            pltpu.VMEM((48, depth), bf),
            dma((4,)), dma((4,)), dma((6,)), dma((6,)), dma((3,)), dma((3,)),
            dma((15,)), dma((15,)), dma, dma,
        ],
        compiler_params=pltpu.CompilerParams(collective_id=0, has_side_effects=True),
    )(feat, cot, mask, pos, weight)


def shards(features, occupancy, brick_pos, weight, cotangent):
    channels = weight.shape[0]
    w2 = weight.transpose(1, 0, 2).reshape(27 * channels, channels)
    output, x_grad, total = fused(
        features[0, 0, 0], cotangent[0, 0, 0], occupancy[0, 0], brick_pos[0, 0], w2
    )
    mine = lax.dynamic_slice(total, (0, lax.axis_index("gy") % 2 * 6, 0), (2, 6, 16 * HALF))
    mine = mine.reshape(2, 6, HALF, 16)[:, :, :, :12].transpose(3, 0, 2, 1)
    w_grad = mine.reshape(12, 2 * HALF, 6)[:, :27] / (lax.axis_size("gx") * lax.axis_size("gy"))
    return (output[None, None, None], x_grad[None, None, None], w_grad)


def solution(mesh):
    placed = (
        P("gx", "gy", None, None, None),
        P("gx", "gy", None, None),
        P("gx", "gy", None),
        P(),
        P("gx", "gy", None, None, None),
    )
    return jax.shard_map(
        shards,
        mesh=mesh,
        in_specs=placed,
        out_specs=(
            P("gx", "gy", None, None, None),
            P("gx", "gy", None, None, None),
            P("gx", None, "gy"),
        ),
        check_vma=False,
    )
```

```python
import jax
import jax.numpy as jnp
from jax import lax
from jax.experimental import pallas as pl
from jax.experimental.pallas import tpu as pltpu
from jax.sharding import PartitionSpec as P

MESH = pl.DeviceIdType.MESH
HALF = 14
BE = 8
TY = 2


def shifted(win, zs, odd):
    flat = win[...].reshape(800, 256)
    row = lax.broadcasted_iota(jnp.int32, flat.shape, 0) & 7
    below = jnp.where(row == 0, 0.0, pltpu.roll(flat, 1, 0))
    above = jnp.where(row == 7, 0.0, pltpu.roll(flat, 799, 0))
    for c, value in enumerate((below, flat, above)):
        zs[c] = value.reshape(10, 10, 8, 256)
        odd[c] = pltpu.roll(value, 64, 1).reshape(10, 10, 8, 256)


def tap_view(ref, tap, flip):
    a, b, c = tap // 9, tap // 3 % 3, tap % 3
    if flip:
        a, b, c = 2 - a, 2 - b, 2 - c
    return ref[c, a : a + BE, b : b + BE].reshape(512, 256)


def fill_columns(cols, zs, odd, flip):
    for pair in range(HALF):
        at = 384 * pair
        even = tap_view(zs, 2 * pair, flip)
        cols[:, at : at + 128] = even[:, :128].astype(jnp.bfloat16)
        if pair < HALF - 1:
            late = tap_view(odd, 2 * pair + 1, flip)
            cols[:, at + 128 : at + 256] = (even[:, 128:] + late[:, :128]).astype(jnp.bfloat16)
            cols[:, at + 256 : at + 384] = late[:, 128:].astype(jnp.bfloat16)
        else:
            cols[:, at + 128 : at + 256] = even[:, 128:].astype(jnp.bfloat16)
            cols[:, at + 256 : at + 384] = jnp.zeros((512, 128), jnp.bfloat16)


def dot_nt(left, right):
    return lax.dot_general(
        left, right, (((1,), (1,)), ((), ())), preferred_element_type=jnp.float32
    )


def halo_sends(own, coef, face_tx, line_tx):
    grid = own.reshape(BE, BE, BE, 256)
    faces = (grid[7], grid[0], grid[:, 7], grid[:, 0])
    for d, face in enumerate(faces):
        flat = face.reshape(64, 256)
        both = jnp.concatenate(
            [flat * coef[2 * d], flat * coef[2 * d + 1]], axis=0
        )
        face_tx[d] = both.astype(jnp.bfloat16)
    lines = (grid[7, 7], grid[7, 0], grid[0, 7], grid[0, 0])
    for d, line in enumerate(lines):
        line = line * coef[8 + d]
        line_tx[d] = jnp.concatenate([line, jnp.zeros_like(line)], axis=0).astype(jnp.bfloat16)


def fill_ring(win, coef, face_rx, line_rx):
    px0, px1, py0, py1 = coef[12:16]
    xm, xp, ym, yp = (
        face_rx[d].astype(jnp.float32).reshape(16, BE, 256) for d in range(4)
    )
    mm, mp, pm, pp = (line_rx[d].astype(jnp.float32)[:BE] for d in range(4))
    win[0, 1:9] = px0 * (py0 * xm[:8] + py1 * xm[8:])
    win[9, 1:9] = px1 * (py0 * xp[:8] + py1 * xp[8:])
    win[1:9, 0] = py0 * (px0 * ym[:8] + px1 * ym[8:])
    win[1:9, 9] = py1 * (px0 * yp[:8] + px1 * yp[8:])
    win[0, 0] = py0 * (px0 * mm + px1 * ym[7]) + py1 * (px0 * xm[7])
    win[9, 0] = py0 * (px0 * ym[8] + px1 * pm) + py1 * (px1 * xp[7])
    win[0, 9] = py1 * (px0 * mp + px1 * yp[7]) + py0 * (px0 * xm[8])
    win[9, 9] = py1 * (px0 * yp[8] + px1 * pp) + py0 * (px1 * xp[8])


def voxel_major(value):
    channels, voxels = value.shape
    return jnp.concatenate([value, jnp.zeros((256 - channels, voxels), jnp.float32)], axis=0).T


def coefficients(pos, gx, gy, nx, ny):
    one = jnp.float32(1.0)
    px, py = (pos >> 1).astype(jnp.float32), (pos & 1).astype(jnp.float32)
    qx, qy = one - px, one - py
    out_x = px * (gx < nx - 1).astype(jnp.float32)
    in_x = qx * (gx > 0).astype(jnp.float32)
    out_y = py * (gy < ny - 1).astype(jnp.float32)
    in_y = qy * (gy > 0).astype(jnp.float32)
    return (
        out_x * qy, out_x * py, in_x * qy, in_x * py,
        out_y * qx, out_y * px, in_y * qx, in_y * px,
        out_x * out_y, out_x * in_y, in_x * out_y, in_x * in_y,
        qx, px, qy, py,
    )


VMEM_SPEC = pl.BlockSpec(memory_space=pltpu.VMEM)
HBM_SPEC = pl.BlockSpec(memory_space=pltpu.HBM)
SMEM_SPEC = pl.BlockSpec(memory_space=pltpu.SMEM)


def fused_kernel(
    feat, cot_hbm, mask, pos, weight_hbm, output_hbm, x_grad_hbm, out, cot, weight, output, x_grad,
    local, win, zs, odd, cols, packed, part,
    face_tx, line_tx, face_rx, line_rx, core_rx, mid, x_rx, acc, yb, y_rx, flat, rows, turned,
    zb, z_rx, face_send, face_recv, line_send, line_recv,
    relay, core_send, core_recv, x_send, x_recv, y_send, y_recv, z_send, z_recv, fin_send, fin_recv,
):
    gx, gy = lax.axis_index("gx"), lax.axis_index("gy")
    x, y = lax.div(gx, 4), lax.rem(gx, 4)
    q, core = lax.div(gy, 2), lax.rem(gy, 2)
    other = 1 - core
    partner = (gx, 2 * q + other)
    x_of = [lax.rem(x + k, 4) for k in range(4)]
    y_of = [lax.rem(y + k, 4) for k in range(4)]
    q_of = [lax.rem(q + k, 16) for k in range(16)]
    x_peer = [(4 * x_of[k] + y, gy) for k in range(4)]
    y_peer = [(4 * x + y_of[k], gy) for k in range(4)]
    q_peer = [(gx, 2 * q_of[k] + core) for k in range(16)]

    nx, ny = lax.axis_size("gx"), lax.axis_size("gy")
    gx_up, gx_down = lax.rem(gx + 1, nx), lax.rem(gx + nx - 1, nx)
    gy_up, gy_down = lax.rem(gy + 1, ny), lax.rem(gy + ny - 1, ny)
    face_peer = [(gx_up, gy), (gx_down, gy), (gx, gy_up), (gx, gy_down)]
    line_peer = [(gx_up, gy_up), (gx_up, gy_down), (gx_down, gy_up), (gx_down, gy_down)]

    load_weight = pltpu.make_async_copy(weight_hbm, weight, local.at[0])
    load_cot = pltpu.make_async_copy(cot_hbm, cot, local.at[1])
    save_output = pltpu.make_async_copy(output, output_hbm, local.at[2])
    save_x_grad = pltpu.make_async_copy(x_grad, x_grad_hbm, local.at[3])
    load_weight.start()
    load_cot.start()
    coef = coefficients(pos[0], gx, gy, nx, ny)

    barrier = pltpu.get_barrier_semaphore()
    peers = [partner] + x_peer[1:] + y_peer[1:] + q_peer[1:] + face_peer + line_peer
    for peer in peers:
        pl.semaphore_signal(barrier, inc=1, device_id=peer, device_id_type=MESH)
    pl.semaphore_wait(barrier, len(peers))

    def remote(src, dst, send, recv, peer):
        return pltpu.make_async_remote_copy(
            src_ref=src, dst_ref=dst, send_sem=send, recv_sem=recv,
            device_id=peer, device_id_type=MESH,
        )

    def halo(step):
        copies = []
        for d in range(4):
            copies.append(
                remote(
                    face_tx.at[step, d], face_rx.at[step, d],
                    face_send.at[step, d], face_recv.at[step, d], face_peer[d],
                )
            )
            copies.append(
                remote(
                    line_tx.at[step, d], line_rx.at[step, d],
                    line_send.at[step, d], line_recv.at[step, d], line_peer[d],
                )
            )
        return copies

    keep = mask[...].astype(jnp.float32)
    bf, f32 = jnp.bfloat16, jnp.float32
    channels = feat.shape[0]
    x_halo, g_halo = halo(0), halo(1)
    own = voxel_major(feat[...].astype(f32) * keep)
    halo_sends(own, coef, face_tx.at[0], line_tx.at[0])
    for copy in x_halo:
        copy.start()
    win[1:9, 1:9] = own.reshape(BE, BE, BE, 256)
    load_weight.wait()
    for pair in range(HALF):
        at = 2 * pair * channels
        left = weight[at : at + channels, :]
        if pair < HALF - 1:
            right = weight[at + channels : at + 2 * channels, :]
        else:
            right = jnp.zeros((channels, channels), bf)
        packed[:, at : at + 2 * channels] = jnp.concatenate([left, right], axis=1)
    for copy in x_halo:
        copy.wait_recv()
    fill_ring(win, coef, face_rx.at[0], line_rx.at[0])
    shifted(win, zs, odd)
    fill_columns(cols, zs, odd, False)
    pre = dot_nt(packed[...], cols[...])
    sigma = 1.0 / (1.0 + jnp.exp(-pre))
    output[...] = (pre * sigma * keep).astype(bf)
    save_output.start()
    load_cot.wait()
    slope = sigma * (1.0 + pre * (1.0 - sigma))
    g = (cot[...].astype(f32) * slope * keep).astype(bf)
    depth = part.shape[3]

    def partial(half):
        view = cols[:, pl.ds(pl.multiple_of(half * depth, 128), depth)]
        grad = jnp.dot(g, view, preferred_element_type=f32)
        part[half] = grad.astype(bf).reshape(part.shape[1:])

    partial(other)
    order = (2, 1, 3, 0)
    core_copy = {
        k: remote(
            part.at[other, x_of[k]], core_rx.at[x_of[k]], core_send.at[k], core_recv.at[k], partner
        )
        for k in order
    }
    for k in order:
        core_copy[k].start()
    own = voxel_major(g.astype(f32))
    halo_sends(own, coef, face_tx.at[1], line_tx.at[1])
    for copy in g_halo:
        copy.start()
    win[1:9, 1:9] = own.reshape(BE, BE, BE, 256)
    partial(core)
    depth = part.shape[3]
    cut = 1408
    lanes_a, lanes_b = pl.ds(0, cut), pl.ds(cut, depth - cut)
    far, right, left = x_of[2], x_of[1], x_of[3]
    routes = (
        (mid.at[far, :, lanes_a], relay.at[:, lanes_a], x_peer[1]),
        (mid.at[far, :, lanes_b], relay.at[:, lanes_b], x_peer[3]),
        (mid.at[right, :, lanes_b], x_rx.at[0, :, lanes_b], x_peer[1]),
        (mid.at[left, :, lanes_a], x_rx.at[1, :, lanes_a], x_peer[3]),
        (mid.at[right, :, lanes_a], x_rx.at[0, :, lanes_a], x_peer[1]),
        (mid.at[left, :, lanes_b], x_rx.at[1, :, lanes_b], x_peer[3]),
    )
    x_copy = [
        remote(src, dst, x_send.at[n], x_recv.at[n], peer)
        for n, (src, dst, peer) in enumerate(routes)
    ]

    def pair_sum(d, lanes):
        return part[core, d, :, lanes].astype(f32) + core_rx[d, :, lanes].astype(f32)

    acc[48:56, :] = jnp.zeros((8, acc.shape[1]), jnp.float32)
    rows[...] = jnp.zeros(rows.shape, jnp.float32)
    for k in order:
        core_copy[k].wait_recv()
        if k == 2:
            mid[far] = pair_sum(far, slice(None)).astype(bf)
            x_copy[0].start()
            x_copy[1].start()
        elif k == 1:
            mid[right, :, lanes_b] = pair_sum(right, lanes_b).astype(bf)
            x_copy[2].start()
        elif k == 3:
            mid[left, :, lanes_a] = pair_sum(left, lanes_a).astype(bf)
            x_copy[3].start()
        else:
            acc[0:48, :] = pair_sum(x, slice(None))
    for copy in g_halo:
        copy.wait_recv()
    fill_ring(win, coef, face_rx.at[1], line_rx.at[1])
    shifted(win, zs, odd)
    x_copy[0].wait_recv()
    relayed = pair_sum(right, lanes_a) + relay[:, lanes_a].astype(f32)
    mid[right, :, lanes_a] = relayed.astype(bf)
    x_copy[4].start()
    x_copy[1].wait_recv()
    relayed = pair_sum(left, lanes_b) + relay[:, lanes_b].astype(f32)
    mid[left, :, lanes_b] = relayed.astype(bf)
    x_copy[5].start()
    fill_columns(cols, zs, odd, True)
    cut, end = 26 * channels, 27 * channels
    back = jnp.dot(cols[:, :cut], weight[:cut, :], preferred_element_type=f32)
    back = back + jnp.dot(cols[:, cut:end], weight[cut:end, :], preferred_element_type=f32)
    wide = jnp.concatenate([back, jnp.zeros((512, 256 - channels), f32)], axis=1)
    x_grad[...] = (wide.T[:channels] * keep).astype(bf)
    save_x_grad.start()
    for n in (2, 3, 4, 5):
        x_copy[n].wait_recv()
    acc[0:48, :] += x_rx[0].astype(f32) + x_rx[1].astype(f32)
    for j in range(4):
        yb[j] = acc[12 * j : 12 * j + 16, :].astype(jnp.bfloat16)
    y_copy = {
        k: remote(yb.at[y_of[k]], y_rx.at[k - 1], y_send.at[k - 1], y_recv.at[k - 1], y_peer[k])
        for k in (2, 1, 3)
    }
    for k in (2, 1, 3):
        y_copy[k].start()
    total = yb[y].astype(jnp.float32)
    for k in (1, 3, 2):
        y_copy[k].wait_recv()
        total = total + y_rx[k - 1].astype(jnp.float32)
    flat[...] = total
    width = flat.shape[1] // HALF
    for t in range(HALF):
        rows[16 * t : 16 * t + 16, 0:width] = flat[:, width * t : width * t + width]
    turned[...] = rows[...].T
    for j in range(16):
        zb[j] = turned[12 * j : 12 * j + 16, :].astype(jnp.bfloat16)
    z_copy = [
        remote(zb.at[q_of[k]], z_rx.at[k - 1], z_send.at[k - 1], z_recv.at[k - 1], q_peer[k])
        for k in range(1, 16)
    ]
    for copy in z_copy:
        copy.start()
    total = zb[q].astype(jnp.float32)
    for k, copy in enumerate(z_copy):
        copy.wait_recv()
        total = total + z_rx[k].astype(jnp.float32)
    out[core] = total
    last = remote(out.at[core], out.at[core], fin_send, fin_recv, partner)
    last.start()
    for k in order:
        core_copy[k].wait_send()
    for copy in x_copy:
        copy.wait_send()
    for k in (2, 1, 3):
        y_copy[k].wait_send()
    for copy in z_copy:
        copy.wait_send()
    for copy in x_halo + g_halo:
        copy.wait_send()
    last.wait()
    save_output.wait()
    save_x_grad.wait()


def fused(feat, cot, mask, pos, weight):
    channels, voxels = feat.shape
    depth = HALF * channels
    bf, f32 = jnp.bfloat16, jnp.float32
    dma = pltpu.SemaphoreType.DMA
    plane = jax.ShapeDtypeStruct((channels, voxels), bf)
    return pl.pallas_call(
        fused_kernel,
        out_shape=(plane, plane, jax.ShapeDtypeStruct((2, 16, 256), f32)),
        in_specs=[VMEM_SPEC, HBM_SPEC, VMEM_SPEC, SMEM_SPEC, HBM_SPEC],
        out_specs=(HBM_SPEC, HBM_SPEC, VMEM_SPEC),
        scratch_shapes=[
            pltpu.VMEM((channels, voxels), bf),
            pltpu.VMEM(weight.shape, bf),
            pltpu.VMEM((channels, voxels), bf),
            pltpu.VMEM((channels, voxels), bf),
            dma((4,)),
            pltpu.VMEM((10, 10, BE, 256), f32),
            pltpu.VMEM((3, 10, 10, BE, 256), f32),
            pltpu.VMEM((3, 10, 10, BE, 256), f32),
            pltpu.VMEM((voxels, 2 * depth), bf),
            pltpu.VMEM((channels, 2 * depth), bf),
            pltpu.VMEM((2, 4, 48, depth), bf),
            pltpu.VMEM((2, 4, 128, 256), bf),
            pltpu.VMEM((2, 4, 16, 256), bf),
            pltpu.VMEM((2, 4, 128, 256), bf),
            pltpu.VMEM((2, 4, 16, 256), bf),
            pltpu.VMEM((4, 48, depth), bf),
            pltpu.VMEM((4, 48, depth), bf),
            pltpu.VMEM((2, 48, depth), bf),
            pltpu.VMEM((56, depth), f32),
            pltpu.VMEM((4, 16, depth), bf),
            pltpu.VMEM((3, 16, depth), bf),
            pltpu.VMEM((16, depth), f32),
            pltpu.VMEM((256, 256), f32),
            pltpu.VMEM((256, 256), f32),
            pltpu.VMEM((16, 16, 256), bf),
            pltpu.VMEM((15, 16, 256), bf),
            dma((2, 4)), dma((2, 4)), dma((2, 4)), dma((2, 4)),
            pltpu.VMEM((48, depth), bf),
            dma((4,)), dma((4,)), dma((6,)), dma((6,)), dma((3,)), dma((3,)),
            dma((15,)), dma((15,)), dma, dma,
        ],
        compiler_params=pltpu.CompilerParams(collective_id=0, has_side_effects=True),
    )(feat, cot, mask, pos, weight)


def finish_kernel(first, second, first_out, second_out, sems):
    copies = [
        pltpu.make_async_copy(first, first_out, sems.at[0]),
        pltpu.make_async_copy(second, second_out, sems.at[1]),
    ]
    for copy in copies:
        copy.start()
    for copy in copies:
        copy.wait()


def finish(first, second):
    return pl.pallas_call(
        finish_kernel,
        out_shape=(
            jax.ShapeDtypeStruct(first.shape, first.dtype),
            jax.ShapeDtypeStruct(second.shape, second.dtype),
        ),
        in_specs=[HBM_SPEC] * 2,
        out_specs=(HBM_SPEC,) * 2,
        scratch_shapes=[pltpu.SemaphoreType.DMA((2,))],
    )(first, second)


def shards(features, occupancy, brick_pos, weight, cotangent):
    channels = weight.shape[0]
    w2 = weight.transpose(1, 0, 2).reshape(27 * channels, channels)
    output, x_grad, total = fused(
        features[0, 0, 0], cotangent[0, 0, 0], occupancy[0, 0], brick_pos[0, 0], w2
    )
    output, x_grad = finish(output, x_grad)
    mine = lax.dynamic_slice(total, (0, lax.axis_index("gy") % 2 * 6, 0), (2, 6, 16 * HALF))
    mine = mine.reshape(2, 6, HALF, 16)[:, :, :, :12].transpose(3, 0, 2, 1)
    w_grad = mine.reshape(12, 2 * HALF, 6)[:, :27] / (lax.axis_size("gx") * lax.axis_size("gy"))
    return (output[None, None, None], x_grad[None, None, None], w_grad)


def solution(mesh):
    placed = (
        P("gx", "gy", None, None, None),
        P("gx", "gy", None, None),
        P("gx", "gy", None),
        P(),
        P("gx", "gy", None, None, None),
    )
    return jax.shard_map(
        shards,
        mesh=mesh,
        in_specs=placed,
        out_specs=(
            P("gx", "gy", None, None, None),
            P("gx", "gy", None, None, None),
            P("gx", None, "gy"),
        ),
        check_vma=False,
    )
```

```python
import jax
import jax.numpy as jnp
from jax import lax
from jax.experimental import pallas as pl
from jax.experimental.pallas import tpu as pltpu
from jax.sharding import PartitionSpec as P

MESH = pl.DeviceIdType.MESH
HALF = 14
BE = 8
TY = 2


def shifted(win, zs, odd):
    flat = win[...].reshape(800, 256)
    row = lax.broadcasted_iota(jnp.int32, flat.shape, 0) & 7
    below = jnp.where(row == 0, 0.0, pltpu.roll(flat, 1, 0))
    above = jnp.where(row == 7, 0.0, pltpu.roll(flat, 799, 0))
    for c, value in enumerate((below, flat, above)):
        zs[c] = value.reshape(10, 10, 8, 256)
        odd[c] = pltpu.roll(value, 64, 1).reshape(10, 10, 8, 256)


def tap_view(ref, tap, flip):
    a, b, c = tap // 9, tap // 3 % 3, tap % 3
    if flip:
        a, b, c = 2 - a, 2 - b, 2 - c
    return ref[c, a : a + BE, b : b + BE].reshape(512, 256)


def fill_columns(cols, zs, odd, flip):
    for pair in range(HALF):
        at = 384 * pair
        even = tap_view(zs, 2 * pair, flip)
        cols[:, at : at + 128] = even[:, :128].astype(jnp.bfloat16)
        if pair < HALF - 1:
            late = tap_view(odd, 2 * pair + 1, flip)
            cols[:, at + 128 : at + 256] = (even[:, 128:] + late[:, :128]).astype(jnp.bfloat16)
            cols[:, at + 256 : at + 384] = late[:, 128:].astype(jnp.bfloat16)
        else:
            cols[:, at + 128 : at + 256] = even[:, 128:].astype(jnp.bfloat16)
            cols[:, at + 256 : at + 384] = jnp.zeros((512, 128), jnp.bfloat16)


def dot_nt(left, right):
    return lax.dot_general(
        left, right, (((1,), (1,)), ((), ())), preferred_element_type=jnp.float32
    )


def halo_sends(own, coef, face_tx, line_tx):
    grid = own.reshape(BE, BE, BE, 256)
    faces = (grid[7], grid[0], grid[:, 7], grid[:, 0])
    for d, face in enumerate(faces):
        flat = face.reshape(64, 256)
        both = jnp.concatenate(
            [flat * coef[2 * d], flat * coef[2 * d + 1]], axis=0
        )
        face_tx[d] = both.astype(jnp.bfloat16)
    lines = (grid[7, 7], grid[7, 0], grid[0, 7], grid[0, 0])
    for d, line in enumerate(lines):
        line = line * coef[8 + d]
        line_tx[d] = jnp.concatenate([line, jnp.zeros_like(line)], axis=0).astype(jnp.bfloat16)


def fill_ring(win, coef, face_rx, line_rx):
    px0, px1, py0, py1 = coef[12:16]
    xm, xp, ym, yp = (
        face_rx[d].astype(jnp.float32).reshape(16, BE, 256) for d in range(4)
    )
    mm, mp, pm, pp = (line_rx[d].astype(jnp.float32)[:BE] for d in range(4))
    win[0, 1:9] = px0 * (py0 * xm[:8] + py1 * xm[8:])
    win[9, 1:9] = px1 * (py0 * xp[:8] + py1 * xp[8:])
    win[1:9, 0] = py0 * (px0 * ym[:8] + px1 * ym[8:])
    win[1:9, 9] = py1 * (px0 * yp[:8] + px1 * yp[8:])
    win[0, 0] = py0 * (px0 * mm + px1 * ym[7]) + py1 * (px0 * xm[7])
    win[9, 0] = py0 * (px0 * ym[8] + px1 * pm) + py1 * (px1 * xp[7])
    win[0, 9] = py1 * (px0 * mp + px1 * yp[7]) + py0 * (px0 * xm[8])
    win[9, 9] = py1 * (px0 * yp[8] + px1 * pp) + py0 * (px1 * xp[8])


def voxel_major(value):
    channels, voxels = value.shape
    return jnp.concatenate([value, jnp.zeros((256 - channels, voxels), jnp.float32)], axis=0).T


def coefficients(pos, gx, gy, nx, ny):
    one = jnp.float32(1.0)
    px, py = (pos >> 1).astype(jnp.float32), (pos & 1).astype(jnp.float32)
    qx, qy = one - px, one - py
    out_x = px * (gx < nx - 1).astype(jnp.float32)
    in_x = qx * (gx > 0).astype(jnp.float32)
    out_y = py * (gy < ny - 1).astype(jnp.float32)
    in_y = qy * (gy > 0).astype(jnp.float32)
    return (
        out_x * qy, out_x * py, in_x * qy, in_x * py,
        out_y * qx, out_y * px, in_y * qx, in_y * px,
        out_x * out_y, out_x * in_y, in_x * out_y, in_x * in_y,
        qx, px, qy, py,
    )


VMEM_SPEC = pl.BlockSpec(memory_space=pltpu.VMEM)
HBM_SPEC = pl.BlockSpec(memory_space=pltpu.HBM)
SMEM_SPEC = pl.BlockSpec(memory_space=pltpu.SMEM)


def fused_kernel(
    feat, cot_hbm, mask, pos, weight_hbm, output_hbm, x_grad_hbm, out, cot, weight, output, x_grad,
    local, win, zs, odd, cols, packed, part,
    face_tx, line_tx, face_rx, line_rx, core_rx, mid, x_rx, acc, yb, y_rx, flat, rows, turned,
    zb, z_rx, face_send, face_recv, line_send, line_recv,
    relay, core_send, core_recv, x_send, x_recv, y_send, y_recv, z_send, z_recv, fin_send, fin_recv,
):
    gx, gy = lax.axis_index("gx"), lax.axis_index("gy")
    x, y = lax.div(gx, 4), lax.rem(gx, 4)
    q, core = lax.div(gy, 2), lax.rem(gy, 2)
    other = 1 - core
    partner = (gx, 2 * q + other)
    x_of = [lax.rem(x + k, 4) for k in range(4)]
    y_of = [lax.rem(y + k, 4) for k in range(4)]
    q_of = [lax.rem(q + k, 16) for k in range(16)]
    x_peer = [(4 * x_of[k] + y, gy) for k in range(4)]
    y_peer = [(4 * x + y_of[k], gy) for k in range(4)]
    q_peer = [(gx, 2 * q_of[k] + core) for k in range(16)]

    nx, ny = lax.axis_size("gx"), lax.axis_size("gy")
    gx_up, gx_down = lax.rem(gx + 1, nx), lax.rem(gx + nx - 1, nx)
    gy_up, gy_down = lax.rem(gy + 1, ny), lax.rem(gy + ny - 1, ny)
    face_peer = [(gx_up, gy), (gx_down, gy), (gx, gy_up), (gx, gy_down)]
    line_peer = [(gx_up, gy_up), (gx_up, gy_down), (gx_down, gy_up), (gx_down, gy_down)]

    load_weight = pltpu.make_async_copy(weight_hbm, weight, local.at[0])
    load_cot = pltpu.make_async_copy(cot_hbm, cot, local.at[1])
    save_output = pltpu.make_async_copy(output, output_hbm, local.at[2])
    save_x_grad = pltpu.make_async_copy(x_grad, x_grad_hbm, local.at[3])
    load_weight.start()
    load_cot.start()
    coef = coefficients(pos[0], gx, gy, nx, ny)

    barrier = pltpu.get_barrier_semaphore()
    peers = [partner] + x_peer[1:] + y_peer[1:] + q_peer[1:] + face_peer + line_peer
    for peer in peers:
        pl.semaphore_signal(barrier, inc=1, device_id=peer, device_id_type=MESH)
    pl.semaphore_wait(barrier, len(peers))

    def remote(src, dst, send, recv, peer):
        return pltpu.make_async_remote_copy(
            src_ref=src, dst_ref=dst, send_sem=send, recv_sem=recv,
            device_id=peer, device_id_type=MESH,
        )

    def halo(step):
        copies = []
        for d in range(4):
            copies.append(
                remote(
                    face_tx.at[step, d], face_rx.at[step, d],
                    face_send.at[step, d], face_recv.at[step, d], face_peer[d],
                )
            )
            copies.append(
                remote(
                    line_tx.at[step, d], line_rx.at[step, d],
                    line_send.at[step, d], line_recv.at[step, d], line_peer[d],
                )
            )
        return copies

    keep = mask[...].astype(jnp.float32)
    bf, f32 = jnp.bfloat16, jnp.float32
    channels = feat.shape[0]
    x_halo, g_halo = halo(0), halo(1)
    own = voxel_major(feat[...].astype(f32) * keep)
    halo_sends(own, coef, face_tx.at[0], line_tx.at[0])
    for copy in x_halo:
        copy.start()
    win[1:9, 1:9] = own.reshape(BE, BE, BE, 256)
    load_weight.wait()
    for pair in range(HALF):
        at = 2 * pair * channels
        left = weight[at : at + channels, :]
        if pair < HALF - 1:
            right = weight[at + channels : at + 2 * channels, :]
        else:
            right = jnp.zeros((channels, channels), bf)
        packed[:, at : at + 2 * channels] = jnp.concatenate([left, right], axis=1)
    for copy in x_halo:
        copy.wait_recv()
    fill_ring(win, coef, face_rx.at[0], line_rx.at[0])
    shifted(win, zs, odd)
    fill_columns(cols, zs, odd, False)
    pre = dot_nt(packed[...], cols[...])
    sigma = 1.0 / (1.0 + jnp.exp(-pre))
    output[...] = (pre * sigma * keep).astype(bf)
    save_output.start()
    load_cot.wait()
    slope = sigma * (1.0 + pre * (1.0 - sigma))
    g = (cot[...].astype(f32) * slope * keep).astype(bf)
    own = voxel_major(g.astype(f32))
    halo_sends(own, coef, face_tx.at[1], line_tx.at[1])
    for copy in g_halo:
        copy.start()
    win[1:9, 1:9] = own.reshape(BE, BE, BE, 256)
    depth = part.shape[3]

    def partial(half):
        view = cols[:, pl.ds(pl.multiple_of(half * depth, 128), depth)]
        grad = jnp.dot(g, view, preferred_element_type=f32)
        part[half] = grad.astype(bf).reshape(part.shape[1:])

    partial(other)
    order = (2, 1, 3, 0)
    core_copy = {
        k: remote(
            part.at[other, x_of[k]], core_rx.at[x_of[k]], core_send.at[k], core_recv.at[k], partner
        )
        for k in order
    }
    for k in order:
        core_copy[k].start()
    partial(core)
    depth = part.shape[3]
    cut = 1408
    lanes_a, lanes_b = pl.ds(0, cut), pl.ds(cut, depth - cut)
    far, right, left = x_of[2], x_of[1], x_of[3]
    routes = (
        (mid.at[far, :, lanes_a], relay.at[:, lanes_a], x_peer[1]),
        (mid.at[far, :, lanes_b], relay.at[:, lanes_b], x_peer[3]),
        (mid.at[right, :, lanes_b], x_rx.at[0, :, lanes_b], x_peer[1]),
        (mid.at[left, :, lanes_a], x_rx.at[1, :, lanes_a], x_peer[3]),
        (mid.at[right, :, lanes_a], x_rx.at[0, :, lanes_a], x_peer[1]),
        (mid.at[left, :, lanes_b], x_rx.at[1, :, lanes_b], x_peer[3]),
    )
    x_copy = [
        remote(src, dst, x_send.at[n], x_recv.at[n], peer)
        for n, (src, dst, peer) in enumerate(routes)
    ]

    def pair_sum(d, lanes):
        return part[core, d, :, lanes].astype(f32) + core_rx[d, :, lanes].astype(f32)

    acc[48:56, :] = jnp.zeros((8, acc.shape[1]), jnp.float32)
    rows[...] = jnp.zeros(rows.shape, jnp.float32)
    for k in order:
        core_copy[k].wait_recv()
        if k == 2:
            mid[far] = pair_sum(far, slice(None)).astype(bf)
            x_copy[0].start()
            x_copy[1].start()
        elif k == 1:
            mid[right, :, lanes_b] = pair_sum(right, lanes_b).astype(bf)
            x_copy[2].start()
        elif k == 3:
            mid[left, :, lanes_a] = pair_sum(left, lanes_a).astype(bf)
            x_copy[3].start()
        else:
            acc[0:48, :] = pair_sum(x, slice(None))
    for copy in g_halo:
        copy.wait_recv()
    fill_ring(win, coef, face_rx.at[1], line_rx.at[1])
    shifted(win, zs, odd)
    x_copy[0].wait_recv()
    relayed = pair_sum(right, lanes_a) + relay[:, lanes_a].astype(f32)
    mid[right, :, lanes_a] = relayed.astype(bf)
    x_copy[4].start()
    x_copy[1].wait_recv()
    relayed = pair_sum(left, lanes_b) + relay[:, lanes_b].astype(f32)
    mid[left, :, lanes_b] = relayed.astype(bf)
    x_copy[5].start()
    fill_columns(cols, zs, odd, True)
    cut, end = 26 * channels, 27 * channels
    back = jnp.dot(cols[:, :cut], weight[:cut, :], preferred_element_type=f32)
    back = back + jnp.dot(cols[:, cut:end], weight[cut:end, :], preferred_element_type=f32)
    wide = jnp.concatenate([back, jnp.zeros((512, 256 - channels), f32)], axis=1)
    x_grad[...] = (wide.T[:channels] * keep).astype(bf)
    save_x_grad.start()
    for n in (2, 3, 4, 5):
        x_copy[n].wait_recv()
    acc[0:48, :] += x_rx[0].astype(f32) + x_rx[1].astype(f32)
    for j in range(4):
        yb[j] = acc[12 * j : 12 * j + 16, :].astype(jnp.bfloat16)
    y_copy = {
        k: remote(yb.at[y_of[k]], y_rx.at[k - 1], y_send.at[k - 1], y_recv.at[k - 1], y_peer[k])
        for k in (2, 1, 3)
    }
    for k in (2, 1, 3):
        y_copy[k].start()
    total = yb[y].astype(jnp.float32)
    for k in (1, 3, 2):
        y_copy[k].wait_recv()
        total = total + y_rx[k - 1].astype(jnp.float32)
    flat[...] = total
    width = flat.shape[1] // HALF
    for t in range(HALF):
        rows[16 * t : 16 * t + 16, 0:width] = flat[:, width * t : width * t + width]
    turned[...] = rows[...].T
    for j in range(16):
        zb[j] = turned[12 * j : 12 * j + 16, :].astype(jnp.bfloat16)
    z_copy = [
        remote(zb.at[q_of[k]], z_rx.at[k - 1], z_send.at[k - 1], z_recv.at[k - 1], q_peer[k])
        for k in range(1, 16)
    ]
    for copy in z_copy:
        copy.start()
    total = zb[q].astype(jnp.float32)
    for k, copy in enumerate(z_copy):
        copy.wait_recv()
        total = total + z_rx[k].astype(jnp.float32)
    out[core] = total
    last = remote(out.at[core], out.at[core], fin_send, fin_recv, partner)
    last.start()
    for k in order:
        core_copy[k].wait_send()
    for copy in x_copy:
        copy.wait_send()
    for k in (2, 1, 3):
        y_copy[k].wait_send()
    for copy in z_copy:
        copy.wait_send()
    for copy in x_halo + g_halo:
        copy.wait_send()
    last.wait()
    save_output.wait()
    save_x_grad.wait()


def fused(feat, cot, mask, pos, weight):
    channels, voxels = feat.shape
    depth = HALF * channels
    bf, f32 = jnp.bfloat16, jnp.float32
    dma = pltpu.SemaphoreType.DMA
    plane = jax.ShapeDtypeStruct((channels, voxels), bf)
    return pl.pallas_call(
        fused_kernel,
        out_shape=(plane, plane, jax.ShapeDtypeStruct((2, 16, 256), f32)),
        in_specs=[VMEM_SPEC, HBM_SPEC, VMEM_SPEC, SMEM_SPEC, HBM_SPEC],
        out_specs=(HBM_SPEC, HBM_SPEC, VMEM_SPEC),
        scratch_shapes=[
            pltpu.VMEM((channels, voxels), bf),
            pltpu.VMEM(weight.shape, bf),
            pltpu.VMEM((channels, voxels), bf),
            pltpu.VMEM((channels, voxels), bf),
            dma((4,)),
            pltpu.VMEM((10, 10, BE, 256), f32),
            pltpu.VMEM((3, 10, 10, BE, 256), f32),
            pltpu.VMEM((3, 10, 10, BE, 256), f32),
            pltpu.VMEM((voxels, 2 * depth), bf),
            pltpu.VMEM((channels, 2 * depth), bf),
            pltpu.VMEM((2, 4, 48, depth), bf),
            pltpu.VMEM((2, 4, 128, 256), bf),
            pltpu.VMEM((2, 4, 16, 256), bf),
            pltpu.VMEM((2, 4, 128, 256), bf),
            pltpu.VMEM((2, 4, 16, 256), bf),
            pltpu.VMEM((4, 48, depth), bf),
            pltpu.VMEM((4, 48, depth), bf),
            pltpu.VMEM((2, 48, depth), bf),
            pltpu.VMEM((56, depth), f32),
            pltpu.VMEM((4, 16, depth), bf),
            pltpu.VMEM((3, 16, depth), bf),
            pltpu.VMEM((16, depth), f32),
            pltpu.VMEM((256, 256), f32),
            pltpu.VMEM((256, 256), f32),
            pltpu.VMEM((16, 16, 256), bf),
            pltpu.VMEM((15, 16, 256), bf),
            dma((2, 4)), dma((2, 4)), dma((2, 4)), dma((2, 4)),
            pltpu.VMEM((48, depth), bf),
            dma((4,)), dma((4,)), dma((6,)), dma((6,)), dma((3,)), dma((3,)),
            dma((15,)), dma((15,)), dma, dma,
        ],
        compiler_params=pltpu.CompilerParams(collective_id=0, has_side_effects=True),
    )(feat, cot, mask, pos, weight)


def finish_kernel(first, second, first_out, second_out):
    first_out[...] = first[...]
    second_out[...] = second[...]


def finish(first, second):
    shape = jax.ShapeDtypeStruct(first.shape, first.dtype)
    return pl.pallas_call(
        finish_kernel,
        out_shape=(shape, shape),
        in_specs=[VMEM_SPEC] * 2,
        out_specs=(VMEM_SPEC,) * 2,
    )(first, second)


def shards(features, occupancy, brick_pos, weight, cotangent):
    channels = weight.shape[0]
    w2 = weight.transpose(1, 0, 2).reshape(27 * channels, channels)
    output, x_grad, total = fused(
        features[0, 0, 0], cotangent[0, 0, 0], occupancy[0, 0], brick_pos[0, 0], w2
    )
    output, x_grad = finish(output, x_grad)
    mine = lax.dynamic_slice(total, (0, lax.axis_index("gy") % 2 * 6, 0), (2, 6, 16 * HALF))
    mine = mine.reshape(2, 6, HALF, 16)[:, :, :, :12].transpose(3, 0, 2, 1)
    w_grad = mine.reshape(12, 2 * HALF, 6)[:, :27] / (lax.axis_size("gx") * lax.axis_size("gy"))
    return (output[None, None, None], x_grad[None, None, None], w_grad)


def solution(mesh):
    placed = (
        P("gx", "gy", None, None, None),
        P("gx", "gy", None, None),
        P("gx", "gy", None),
        P(),
        P("gx", "gy", None, None, None),
    )
    return jax.shard_map(
        shards,
        mesh=mesh,
        in_specs=placed,
        out_specs=(
            P("gx", "gy", None, None, None),
            P("gx", "gy", None, None, None),
            P("gx", None, "gy"),
        ),
        check_vma=False,
    )
```
